512 devices in a mesh: dp: 64 (over y, z_hi, core), section: 8 (over x, z_lo).
Axes of the slice: x: 4, y: 8, z: 8 (z_hi: 4, z_lo: 2; z = z_hi * 2 + z_lo), core: 2. Of those that a mesh axis runs over, the one named last changes fastest.
Arguments:
- features: bfloat16 [256, 64, 512], P('dp'), may hold values from -6 to 6
- lengths: int32 [256], P('dp'), may hold values from 32 to 64
- front_weight: bfloat16 [512, 768], replicated, may hold values from -0.25 to 0.25
- pointwise: bfloat16 [8, 768, 768], P('section'), may hold values from -0.21875 to 0.21875
- kernel: float32 [8, 5, 768], P('section'), may hold values from -2.5 to 2.5
- targets: bfloat16 [256, 64, 768], P('dp'), may hold values from -6 to 6
Outputs:
- grad_pointwise: bfloat16 [8, 768, 768], P('section')
- grad_kernel: float32 [8, 5, 768], P('section')
The draws below stay inside these ranges and needn't reach their ends.
All inputs are finite; a program needn't handle non-finite values.
Results may differ from the reference program's by a relative error of at most 0.005.
Values may be sent and summed in bfloat16 or wider, within the bound.
No kernel may reach another device: no remote copies, remote signals or barrier semaphores. Data moves between devices by JAX's collectives and lax.ppermute only.
A program may use at most 64 MiB of HBM per device.

```python
import jax
import jax.numpy as jnp
from jax import lax

D = 768
KER = 5
FEAT = 512
FRAMES = 64
UTTS = 256
LAYERS = 8


def touch_ends(values, rng, low, high):
    spot = [jax.random.randint(jax.random.fold_in(rng, axis), (), 0, length) for axis, length in enumerate(values.shape)]
    widest = values.shape.index(max(values.shape))
    beside = spot[:widest] + [(spot[widest] + 1) % values.shape[widest]] + spot[widest + 1:]
    return values.at[tuple(spot)].set(low).at[tuple(beside)].set(high)


def steps_of(rng, extent, shards, smallest, largest):
    def one(dim, blocks):
        steps = jax.random.uniform(jax.random.fold_in(jax.random.fold_in(rng, 6), dim), (blocks,), jnp.float32, smallest / len(shards), largest / len(shards))
        return jnp.repeat(jnp.exp(steps), extent[dim] // blocks).reshape((-1,) + (1,) * (len(extent) - dim - 1))

    gain = one(*shards[0])
    for cut in shards[1:]:
        gain = gain * one(*cut)
    return gain


def bell_draw(rng, shape, scale, reach, split=(), held_as=jnp.bfloat16):
    result = scale * jax.random.normal(rng, shape, jnp.float32)
    if split:
        result = result * steps_of(rng, shape, split, -0.22, 0.18)
    return jnp.clip(result, -reach, reach).astype(held_as)


def setup_inputs(seed: int = 0) -> dict:
    streams_of = jax.random.split(jax.random.key(seed), 7)
    features = bell_draw(streams_of[0], (UTTS, FRAMES, FEAT), 1.0, 6.0, ((0, 64),))
    lengths = touch_ends(jax.random.randint(streams_of[1], (UTTS,), FRAMES // 2, FRAMES + 1), jax.random.fold_in(streams_of[1], 1), FRAMES // 2, FRAMES).astype(jnp.int32)
    front_weight = bell_draw(streams_of[2], (FEAT, D), FEAT ** -0.5, 0.25)
    pointwise = bell_draw(streams_of[3], (LAYERS, D, D), D ** -0.5, 0.21875, ((0, 8),))
    kernel = bell_draw(streams_of[4], (LAYERS, KER, D), KER ** -0.5, 2.5, ((0, 8),), jnp.float32)
    targets = bell_draw(streams_of[5], (UTTS, FRAMES, D), 1.0, 6.0, ((0, 64),))
    return {"features": features, "lengths": lengths, "front_weight": front_weight, "pointwise": pointwise, "kernel": kernel, "targets": targets}


EPS = 1e-06

def depthwise(signal, taps):
    half_span = taps.shape[0] // 2
    frames = signal.shape[-2]
    padding = [(0, 0)] * (signal.ndim - 2) + [(half_span, half_span), (0, 0)]
    padded = jnp.pad(signal, padding)
    summed = jnp.zeros_like(signal)
    for offset in range(taps.shape[0]):
        summed = summed + taps[offset] * lax.slice_in_dim(padded, offset, offset + frames, axis=signal.ndim - 2)
    return summed

def depthwise_transpose(signal, taps):
    half_span = taps.shape[0] // 2
    frames = signal.shape[-2]
    padding = [(0, 0)] * (signal.ndim - 2) + [(half_span, half_span), (0, 0)]
    padded = jnp.pad(signal, padding)
    summed = jnp.zeros_like(signal)
    for offset in range(taps.shape[0]):
        begin = 2 * half_span - offset
        summed = summed + taps[offset] * lax.slice_in_dim(padded, begin, begin + frames, axis=signal.ndim - 2)
    return summed

def taps_gradient(normed, grad_conv, count):
    half_span = count // 2
    frames = normed.shape[-2]
    padding = [(0, 0)] * (normed.ndim - 2) + [(half_span, half_span), (0, 0)]
    padded = jnp.pad(normed, padding)
    width = normed.shape[-1]
    rows = []
    for offset in range(count):
        window = lax.slice_in_dim(padded, offset, offset + frames, axis=normed.ndim - 2)
        rows.append(lax.optimization_barrier(jnp.sum((grad_conv * window).reshape(-1, width), axis=0)))
    return jnp.stack(rows)

def block_inner(block_input, taps, frame_mask):
    values = block_input.astype(jnp.float32)
    scale_inv = lax.rsqrt(lax.optimization_barrier(jnp.mean(values * values, axis=-1, keepdims=True)) + EPS)
    normed = values * scale_inv * frame_mask[..., None]
    conv_out = depthwise(normed, taps)
    sigmoid_out = jax.nn.sigmoid(conv_out)
    activated = (conv_out * sigmoid_out).astype(jnp.bfloat16)
    return (values, scale_inv, normed, conv_out, sigmoid_out, activated)

def block_forward(block_input, weight, taps, frame_mask):
    values, scale_inv, normed, conv_out, sigmoid_out, activated = block_inner(block_input, taps, frame_mask)
    width = weight.shape[0]
    update = jnp.dot(activated.reshape(-1, width), weight, preferred_element_type=jnp.float32)
    return (values + update.reshape(values.shape)).astype(jnp.bfloat16)

def block_backward(block_input, weight, taps, frame_mask, cotangent):
    values, scale_inv, normed, conv_out, sigmoid_out, activated = block_inner(block_input, taps, frame_mask)
    width = weight.shape[0]
    flat_cot = cotangent.reshape(-1, width)
    grad_weight = jnp.dot(activated.reshape(-1, width).T, flat_cot, preferred_element_type=jnp.float32)
    grad_act = jnp.dot(flat_cot, weight.T, preferred_element_type=jnp.float32).reshape(values.shape)
    grad_conv = grad_act * sigmoid_out * (1.0 + conv_out * (1.0 - sigmoid_out))
    grad_taps = taps_gradient(normed, grad_conv, taps.shape[0])
    grad_normed = depthwise_transpose(grad_conv, taps) * frame_mask[..., None]
    grad_values = scale_inv * grad_normed - values * scale_inv * scale_inv * scale_inv * lax.optimization_barrier(jnp.mean(grad_normed * values, axis=-1, keepdims=True))
    grad_input = (cotangent.astype(jnp.float32) + grad_values).astype(jnp.bfloat16)
    return (grad_input, grad_weight, grad_taps)

def head_gradient(outputs, targets, frame_mask, lengths):
    differ = (outputs.astype(jnp.float32) - targets.astype(jnp.float32)) * frame_mask[..., None]
    return (differ / lengths.astype(jnp.float32)[:, None, None]).astype(jnp.bfloat16)

def reference(features, lengths, front_weight, pointwise, kernel, targets):
    frame_mask = (jnp.arange(FRAMES, dtype=jnp.int32)[None, :] < lengths[:, None]).astype(jnp.float32)
    hidden = jnp.dot(features.reshape(-1, FEAT), front_weight, preferred_element_type=jnp.float32)
    hidden = hidden.reshape(UTTS, FRAMES, D).astype(jnp.bfloat16)
    stored = []
    for layer_index in range(LAYERS):
        stored.append(hidden)
        hidden = block_forward(hidden, pointwise[layer_index], kernel[layer_index], frame_mask)
    cotangent = head_gradient(hidden, targets, frame_mask, lengths)
    weight_grads = [None] * LAYERS
    tap_grads = [None] * LAYERS
    for layer_index in reversed(range(LAYERS)):
        cotangent, grad_weight, grad_taps = block_backward(stored[layer_index], pointwise[layer_index], kernel[layer_index], frame_mask, cotangent)
        weight_grads[layer_index] = grad_weight
        tap_grads[layer_index] = grad_taps
    return (jnp.stack(weight_grads).astype(jnp.bfloat16), jnp.stack(tap_grads))
```

```python
import itertools

import jax
import jax.numpy as jnp
from jax import lax
from jax.experimental import pallas as pl
from jax.experimental.pallas import tpu as pltpu
from jax.sharding import Mesh, PartitionSpec as P

EPS = 1e-06
BF = jnp.bfloat16
F32 = jnp.float32

D = 768
H = 384
KER = 5
FEAT = 512
T = 64
L = 8
TAPS = 16
PIECE = H + TAPS
INROWS = T + 16
PAY = T + T // 2 + TAPS
PEERS = 32
CHUNK = 72
CROWS = 80
MIB = 1024 * 1024

VMEM = pl.BlockSpec(memory_space=pltpu.VMEM)
ANY = pl.BlockSpec(memory_space=pl.ANY)
SMEM = pl.BlockSpec(memory_space=pltpu.SMEM)


def route(shape, step):
    spots = list(itertools.product(*map(range, shape)))
    place = {spot: i for i, spot in enumerate(spots)}
    return [(place[spot], place[step(*spot)]) for spot in spots]


def split3(x):
    hi = x.astype(BF).astype(F32)
    rest = x - hi
    mid = rest.astype(BF).astype(F32)
    return hi, mid, rest - mid


def where_am_i():
    section = 2 * lax.axis_index("x") + lax.axis_index("zl")
    return section, lax.axis_index("c")


def prep_kernel(w_ref, taps_ref, feat_ref, targ_ref, len_ref, near_ref, far_ref, io_ref):
    section, core = where_am_i()
    utt = lax.rem(section, 4)
    hi, mid, low = split3(taps_ref[0])
    packed = jnp.concatenate([hi, mid, low, jnp.zeros((1, D), F32)], axis=0).astype(BF)
    mine = pl.multiple_of(core * H, H)
    theirs = pl.multiple_of((1 - core) * H, H)
    near_ref[0:H, :] = w_ref[0, pl.ds(mine, H), :]
    near_ref[H:PIECE, :] = packed
    far_ref[...] = w_ref[0, pl.ds(theirs, H), :]
    io_ref[0:T, 0:FEAT] = feat_ref[utt]
    io_ref[0:T, FEAT:] = targ_ref[utt]
    count = len_ref[utt].astype(F32)
    io_ref[T:, :] = jnp.full((INROWS - T, FEAT + D), count, F32).astype(BF)


def model_kernel(
    io_a_ref, io_b_ref, front_ref,
    n0, f0, n1, f1, n2, n3, n4, f4, n5, m1, g1, m2, m3, m4, g4, m5,
    pay_ref,
    w_ref, traw_ref, taps_ref, vals_ref, inv_ref, norm_ref, slope_ref, act_ref, gpad_ref, g_ref,
    sem,
):
    section, core = where_am_i()
    col = lax.div(section, 2)
    row = lax.rem(section, 2)
    other = 1 - core
    side = lax.rem(col + 3 + 2 * core, 4)
    anti = lax.rem(col + 1 + 2 * core, 4)
    across = lax.rem(col + 2, 4)
    copies = []

    def bring(piece, c, r, part, with_taps):
        layer = 2 * c + r
        k = len(copies)
        start = pl.multiple_of(part * H, H)
        copies.append(pltpu.make_async_copy(
            piece.at[pl.ds(0, H)], w_ref.at[layer, pl.ds(start, H)], sem.at[k]))
        if with_taps:
            copies.append(pltpu.make_async_copy(
                piece.at[pl.ds(H, TAPS)], traw_ref.at[layer], sem.at[k + 1]))

    flip = 1 - row
    bring(n0, col, row, core, True)
    bring(f0, col, row, other, False)
    bring(n1, side, row, core, True)
    bring(f1, side, row, other, False)
    bring(n2, across, row, core, True)
    bring(n3, col, flip, core, True)
    bring(n4, side, flip, core, True)
    bring(f4, side, flip, other, False)
    bring(n5, across, flip, core, True)
    bring(m1, anti, row, other, True)
    bring(g1, anti, row, core, False)
    bring(m2, across, row, other, False)
    bring(m3, col, flip, other, False)
    bring(m4, anti, flip, other, True)
    bring(g4, anti, flip, core, False)
    bring(m5, across, flip, other, False)
    for copy in copies:
        copy.start()

    own = core == lax.div(section, 4)
    pick = jnp.where(own, 1.0, 0.0).astype(F32)
    io = io_a_ref[...].astype(F32) * pick + io_b_ref[...].astype(F32) * (1.0 - pick)
    count = io[T:T + 1, 0:1]
    target = io[0:T, FEAT:]
    frame = lax.broadcasted_iota(jnp.int32, (T, 1), 0).astype(F32)
    mask = jnp.where(frame < count, 1.0, 0.0).astype(F32)
    hidden = jnp.dot(io[0:T, 0:FEAT].astype(BF), front_ref[...], preferred_element_type=F32)
    g_ref[...] = hidden.astype(BF).astype(F32)

    edge = jnp.zeros((8, D), F32)
    gpad_ref[0:8, :] = edge
    gpad_ref[T + 8:, :] = edge
    for copy in copies:
        copy.wait()

    def forward(l, carry):
        raw = traw_ref[l].astype(F32)
        taps = raw[0:KER] + raw[KER:2 * KER] + raw[2 * KER:3 * KER]
        taps_ref[l, 0:KER, :] = taps
        vals = g_ref[...]
        inv = lax.rsqrt(jnp.mean(vals * vals, axis=-1, keepdims=True) + EPS)
        norm = vals * inv * mask
        vals_ref[l] = vals
        inv_ref[l] = jnp.broadcast_to(inv, (T, 128))
        norm_ref[l, 0:8, :] = edge
        norm_ref[l, T + 8:, :] = edge
        norm_ref[l, 8:T + 8, :] = norm
        conv = taps[0:1] * norm_ref[l, 6:T + 6, :]
        for k in range(1, KER):
            conv = conv + taps[k:k + 1] * norm_ref[l, 6 + k:T + 6 + k, :]
        sig = jax.nn.sigmoid(conv)
        act = (conv * sig).astype(BF)
        slope_ref[l] = sig * (1.0 + conv * (1.0 - sig))
        act_ref[l] = act
        out = vals + jnp.dot(act, w_ref[l], preferred_element_type=F32)
        g_ref[...] = out.astype(BF).astype(F32)
        return carry

    lax.fori_loop(0, L, forward, 0)

    g_ref[...] = ((g_ref[...] - target) * mask / count).astype(BF).astype(F32)

    def backward(i, carry):
        l = L - 1 - i
        g = g_ref[...]
        gb = g.astype(BF)
        pay_ref[l, 0:T, :] = gb
        act = act_ref[l].astype(F32)
        share = jnp.where(core == 0, act[:, 0:H], act[:, H:])
        pay_ref[l, T:T + T // 2, 0:H] = share[0:T // 2].astype(BF)
        pay_ref[l, T:T + T // 2, H:] = share[T // 2:].astype(BF)
        grad_act = lax.dot_general(
            gb, w_ref[l], (((1,), (1,)), ((), ())), preferred_element_type=F32)
        grad_conv = grad_act * slope_ref[l]
        gpad_ref[8:T + 8, :] = grad_conv
        taps = taps_ref[l, 0:KER, :]
        rows = []
        for k in range(KER):
            rows.append(jnp.sum(grad_conv * norm_ref[l, 6 + k:T + 6 + k, :], axis=0, keepdims=True))
        total = jnp.concatenate(rows, axis=0)
        hi = total.astype(BF).astype(F32)
        packed = jnp.concatenate([hi, total - hi, jnp.zeros((TAPS - 2 * KER, D), F32)], axis=0)
        pay_ref[l, T + T // 2:, :] = packed.astype(BF)
        grad_norm = taps[0:1] * gpad_ref[10:T + 10, :]
        for k in range(1, KER):
            grad_norm = grad_norm + taps[k:k + 1] * gpad_ref[10 - k:T + 10 - k, :]
        grad_norm = grad_norm * mask
        vals = vals_ref[l]
        inv = inv_ref[l][:, 0:1]
        mean = jnp.mean(grad_norm * vals, axis=-1, keepdims=True)
        g_ref[...] = (g + (inv * grad_norm - vals * (inv * inv * inv * mean))).astype(BF).astype(F32)
        return carry

    lax.fori_loop(0, L, backward, 0)


def grad_kernel(recv_ref, out_ref, act_ref, flat_ref, row_ref, chunk_ref):
    half = T // 2
    for i in range(L):
        act_ref[i * T:i * T + half, :] = recv_ref[i, T:T + half, 0:H]
        act_ref[i * T + half:(i + 1) * T, :] = recv_ref[i, T:T + half, H:]
    g = recv_ref[:, 0:T, :].reshape(L * T, D)
    grad = lax.dot_general(
        act_ref[...], g, (((0,), (0,)), ((), ())), preferred_element_type=F32)
    for b in range(D // 128):
        flat_ref[b * H:(b + 1) * H, :] = grad[:, b * 128:(b + 1) * 128]
    taps = recv_ref[0, T + half:, :].astype(F32)
    for i in range(1, L):
        taps = taps + recv_ref[i, T + half:, :].astype(F32)
    total = taps[0:KER] + taps[KER:2 * KER]
    hi = total.astype(BF).astype(F32)
    low = total - hi
    chunk_ref[CHUNK:, :] = jnp.zeros((CROWS - CHUNK, 128), F32)
    for j in range(PEERS):
        chunk_ref[0:CHUNK, :] = flat_ref[j * CHUNK:(j + 1) * CHUNK, :]
        if j < KER * 6:
            k, b = divmod(j, 6)
            chunk_ref[CHUNK:CHUNK + 1, :] = hi[k:k + 1, b * 128:(b + 1) * 128]
            chunk_ref[CHUNK + 1:CHUNK + 2, :] = low[k:k + 1, b * 128:(b + 1) * 128]
        out_ref[j] = chunk_ref[...].astype(BF)


def sum_kernel(parts_ref, out_ref, chunk_ref):
    total = parts_ref[0].astype(F32)
    for j in range(1, PEERS):
        total = total + parts_ref[j].astype(F32)
    chunk_ref[...] = total
    tap = total[CHUNK:CHUNK + 1] + total[CHUNK + 1:CHUNK + 2]
    hi = tap.astype(BF).astype(F32)
    chunk_ref[CHUNK:CHUNK + 1, :] = hi
    chunk_ref[CHUNK + 1:CHUNK + 2, :] = tap - hi
    mine = chunk_ref[...].astype(BF)
    for j in range(PEERS):
        out_ref[j] = mine


def place_kernel(mine_ref, theirs_ref, grad_ref, taps_ref, flat_ref):
    core = lax.axis_index("c")
    for ref, which in ((mine_ref, core), (theirs_ref, 1 - core)):
        start = pl.multiple_of(which * H, H)
        for j in range(PEERS):
            flat_ref[j * CHUNK:(j + 1) * CHUNK, :] = ref[j, 0:CHUNK, :].astype(F32)
        for b in range(D // 128):
            grad_ref[0, pl.ds(start, H), b * 128:(b + 1) * 128] = (
                flat_ref[b * H:(b + 1) * H, :].astype(BF))
    for j in range(KER * 6):
        k, b = divmod(j, 6)
        pair = mine_ref[j, CHUNK:, :].astype(F32)
        taps_ref[0, k:k + 1, b * 128:(b + 1) * 128] = pair[0:1] + pair[1:2]


def params(mib):
    return pltpu.CompilerParams(vmem_limit_bytes=mib * MIB)


def body(features, lengths, front_weight, pointwise, kernel, targets):
    ring = route((2, 4), lambda c, x: (c, (x + 1 if c == 0 else x - 1) % 4))
    pair = route(
        (4, 2, 2),
        lambda h, c, z: (h, c, 1 - z) if c == 0 else ((h + 2 * z - 1) % 4, c, 1 - z),
    )

    def along_x(a):
        return lax.ppermute(a, ("c", "x"), ring)

    def along_z(a):
        return lax.ppermute(a, ("zh", "c", "zl"), pair)

    def to_core(a):
        return lax.ppermute(a, "c", [(0, 1), (1, 0)])

    near, far, io = pl.pallas_call(
        prep_kernel,
        name="prep",
        out_shape=(
            jax.ShapeDtypeStruct((PIECE, D), BF),
            jax.ShapeDtypeStruct((H, D), BF),
            jax.ShapeDtypeStruct((INROWS, FEAT + D), BF),
        ),
        in_specs=[VMEM, VMEM, VMEM, VMEM, SMEM],
        out_specs=(VMEM, VMEM, VMEM),
    )(pointwise, kernel, features, targets, lengths)

    n1 = along_x(near)
    n3 = along_z(near)
    f1 = along_x(far)
    io_other = to_core(io)
    n2 = along_x(n1)
    n4 = along_z(n1)
    f4 = along_z(f1)
    n5 = along_z(n2)
    here = [near, far, n1, f1, n2, n3, n4, f4, n5]
    there = [to_core(a) for a in (n1, f1, n2, n3, n4, f4, n5)]

    payload = pl.pallas_call(
        model_kernel,
        name="model",
        out_shape=jax.ShapeDtypeStruct((L, PAY, D), BF),
        in_specs=[VMEM, VMEM, VMEM] + [ANY] * 16,
        out_specs=VMEM,
        scratch_shapes=[
            pltpu.VMEM((L, D, D), BF),
            pltpu.VMEM((L, TAPS, D), BF),
            pltpu.VMEM((L, 8, D), F32),
            pltpu.VMEM((L, T, D), F32),
            pltpu.VMEM((L, T, 128), F32),
            pltpu.VMEM((L, T + 16, D), F32),
            pltpu.VMEM((L, T, D), F32),
            pltpu.VMEM((L, T, D), BF),
            pltpu.VMEM((T + 16, D), F32),
            pltpu.VMEM((T, D), F32),
            pltpu.SemaphoreType.DMA((32,)),
        ],
        compiler_params=params(40),
    )(io, io_other, front_weight, *here, *there)

    received = lax.all_to_all(payload, ("x", "zl"), 0, 0)

    parts = pl.pallas_call(
        grad_kernel,
        name="grad",
        out_shape=jax.ShapeDtypeStruct((PEERS, CROWS, 128), BF),
        in_specs=[VMEM],
        out_specs=VMEM,
        scratch_shapes=[
            pltpu.VMEM((L * T, H), BF),
            pltpu.VMEM((H * 6, 128), F32),
            pltpu.VMEM((8, D), F32),
            pltpu.VMEM((CROWS, 128), F32),
        ],
        compiler_params=params(24),
    )(received)

    scattered = lax.all_to_all(parts, ("y", "zh"), 0, 0)

    mine = pl.pallas_call(
        sum_kernel,
        name="total",
        out_shape=jax.ShapeDtypeStruct((PEERS, CROWS, 128), BF),
        in_specs=[VMEM],
        out_specs=VMEM,
        scratch_shapes=[pltpu.VMEM((CROWS, 128), F32)],
        compiler_params=params(16),
    )(scattered)

    half = lax.all_to_all(mine, ("y", "zh"), 0, 0)
    other_half = to_core(half)

    return pl.pallas_call(
        place_kernel,
        name="place",
        out_shape=(
            jax.ShapeDtypeStruct((1, D, D), BF),
            jax.ShapeDtypeStruct((1, KER, D), F32),
        ),
        in_specs=[VMEM, VMEM],
        out_specs=(VMEM, VMEM),
        scratch_shapes=[pltpu.VMEM((H * 6, 128), F32)],
        compiler_params=params(16),
    )(half, other_half)


def solution(mesh):
    fine = Mesh(mesh.devices.reshape(8, 4, 2, 4, 2), ("y", "zh", "c", "x", "zl"))
    dp = ("y", "zh", "c")
    section = ("x", "zl")
    return jax.shard_map(
        body,
        mesh=fine,
        in_specs=(
            P(dp, None, None),
            P(dp),
            P(),
            P(section, None, None),
            P(section, None, None),
            P(dp, None, None),
        ),
        out_specs=(P(section, None, None), P(section, None, None)),
        check_vma=False,
    )
```

```python
import itertools

import jax
import jax.numpy as jnp
from jax import lax
from jax.experimental import pallas as pl
from jax.experimental.pallas import tpu as pltpu
from jax.sharding import Mesh, PartitionSpec as P

EPS = 1e-06
BF = jnp.bfloat16
F32 = jnp.float32

D = 768
H = 384
KER = 5
FEAT = 512
T = 64
L = 8
TAPS = 16
PIECE = H + TAPS
INROWS = T + 16
PAY = T + T // 2 + TAPS
PEERS = 32
CHUNK = 72
CROWS = 80
MIB = 1024 * 1024

VMEM = pl.BlockSpec(memory_space=pltpu.VMEM)
ANY = pl.BlockSpec(memory_space=pl.ANY)
SMEM = pl.BlockSpec(memory_space=pltpu.SMEM)


def route(shape, step):
    spots = list(itertools.product(*map(range, shape)))
    place = {spot: i for i, spot in enumerate(spots)}
    return [(place[spot], place[step(*spot)]) for spot in spots]


def split3(x):
    hi = x.astype(BF).astype(F32)
    rest = x - hi
    mid = rest.astype(BF).astype(F32)
    return hi, mid, rest - mid


def where_am_i():
    section = 2 * lax.axis_index("x") + lax.axis_index("zl")
    return section, lax.axis_index("c")


def prep_kernel(
    w_ref, taps_ref, feat_ref, targ_ref, len_ref, both_ref, near_ref, io_ref,
    packed_ref, count_ref, sem,
):
    section, core = where_am_i()
    utt = lax.rem(section, 4)
    mine = pl.multiple_of(core * H, H)
    theirs = pl.multiple_of((1 - core) * H, H)
    copies = [
        pltpu.make_async_copy(w_ref.at[0, pl.ds(mine, H)], both_ref.at[pl.ds(0, H)], sem.at[0]),
        pltpu.make_async_copy(w_ref.at[0, pl.ds(theirs, H)], both_ref.at[pl.ds(PIECE, H)], sem.at[1]),
        pltpu.make_async_copy(
            feat_ref.at[utt], io_ref.at[pl.ds(0, T), pl.ds(0, FEAT)], sem.at[2]),
        pltpu.make_async_copy(w_ref.at[0, pl.ds(mine, H)], near_ref.at[pl.ds(0, H)], sem.at[6]),
        pltpu.make_async_copy(
            targ_ref.at[utt], io_ref.at[pl.ds(0, T), pl.ds(FEAT, D)], sem.at[3]),
    ]
    for copy in copies:
        copy.start()
    taps = jnp.concatenate([taps_ref[k] for k in range(KER)], axis=0)
    hi, mid, low = split3(taps)
    packed = jnp.concatenate([hi, mid, low, jnp.zeros((1, D), F32)], axis=0)
    packed_ref[...] = packed.astype(BF)
    count = len_ref[utt].astype(F32)
    count_ref[...] = jnp.full((INROWS - T, FEAT + D), count, F32).astype(BF)
    late = [
        pltpu.make_async_copy(packed_ref, both_ref.at[pl.ds(H, TAPS)], sem.at[4]),
        pltpu.make_async_copy(packed_ref, near_ref.at[pl.ds(H, TAPS)], sem.at[7]),
        pltpu.make_async_copy(count_ref, io_ref.at[pl.ds(T, INROWS - T)], sem.at[5]),
    ]
    for copy in late:
        copy.start()
    for copy in copies + late:
        copy.wait()


def model_kernel(
    io_a_ref, io_b_ref, front_ref,
    own_w, near_w, n3, n2, slant_w, n5, anti_w, m3, m2, far_w, m5,
    pay_ref,
    w_ref, traw_ref, taps_ref, vals_ref, inv_ref, norm_ref, slope_ref, act_ref, gpad_ref, g_ref,
    io_ref, wsem, tsem, isem,
):
    section, core = where_am_i()
    col = lax.div(section, 2)
    row = lax.rem(section, 2)
    other = 1 - core
    side = lax.rem(col + 3 + 2 * core, 4)
    anti = lax.rem(col + 1 + 2 * core, 4)
    across = lax.rem(col + 2, 4)
    flip = 1 - row
    inputs = [
        pltpu.make_async_copy(ref, io_ref.at[i], isem.at[i])
        for i, ref in enumerate((io_a_ref, io_b_ref))
    ]
    for copy in inputs:
        copy.start()

    def bring(piece, first, c, r, part, taps_at):
        layer = 2 * c + r
        start = pl.multiple_of(part * H, H)
        pltpu.make_async_copy(
            piece.at[pl.ds(first, H)], w_ref.at[layer, pl.ds(start, H)], wsem.at[layer]).start()
        if taps_at is not None:
            pltpu.make_async_copy(
                piece.at[pl.ds(taps_at, TAPS)], traw_ref.at[layer], tsem.at[layer]).start()

    for piece, c, r, part in (
        (own_w, col, row, core), (near_w, side, row, core), (slant_w, side, flip, core),
        (anti_w, anti, row, other), (far_w, anti, flip, other),
    ):
        bring(piece, 0, c, r, part, H)
        bring(piece, PIECE, c, r, 1 - part, None)
    for piece, mirror, c, r in (
        (n3, m3, col, flip), (n2, m2, across, row), (n5, m5, across, flip),
    ):
        bring(piece, 0, c, r, core, H)
        bring(mirror, 0, c, r, other, None)

    for copy in inputs:
        copy.wait()
    own = core == lax.div(section, 4)
    pick = jnp.where(own, 1.0, 0.0).astype(F32)
    io = io_ref[0].astype(F32) * pick + io_ref[1].astype(F32) * (1.0 - pick)
    count = io[T:T + 1, 0:1]
    target = io[0:T, FEAT:]
    frame = lax.broadcasted_iota(jnp.int32, (T, 1), 0).astype(F32)
    mask = jnp.where(frame < count, 1.0, 0.0).astype(F32)
    hidden = jnp.dot(io[0:T, 0:FEAT].astype(BF), front_ref[...], preferred_element_type=F32)
    g_ref[...] = hidden.astype(BF).astype(F32)

    edge = jnp.zeros((8, D), F32)
    gpad_ref[0:8, :] = edge
    gpad_ref[T + 8:, :] = edge

    def forward(l, carry):
        pltpu.make_async_copy(traw_ref.at[l], traw_ref.at[l], tsem.at[l]).wait()
        pltpu.make_async_copy(w_ref.at[l], w_ref.at[l], wsem.at[l]).wait()
        raw = traw_ref[l].astype(F32)
        taps = raw[0:KER] + raw[KER:2 * KER] + raw[2 * KER:3 * KER]
        taps_ref[l, 0:KER, :] = taps
        vals = g_ref[...]
        inv = lax.rsqrt(jnp.mean(vals * vals, axis=-1, keepdims=True) + EPS)
        norm = vals * inv * mask
        vals_ref[l] = vals
        inv_ref[l] = jnp.broadcast_to(inv, (T, 128))
        norm_ref[l, 0:8, :] = edge
        norm_ref[l, T + 8:, :] = edge
        norm_ref[l, 8:T + 8, :] = norm
        conv = taps[0:1] * norm_ref[l, 6:T + 6, :]
        for k in range(1, KER):
            conv = conv + taps[k:k + 1] * norm_ref[l, 6 + k:T + 6 + k, :]
        sig = jax.nn.sigmoid(conv)
        act = (conv * sig).astype(BF)
        slope_ref[l] = sig * (1.0 + conv * (1.0 - sig))
        act_ref[l] = act
        out = vals + jnp.dot(act, w_ref[l], preferred_element_type=F32)
        g_ref[...] = out.astype(BF).astype(F32)
        return carry

    lax.fori_loop(0, L, forward, 0)

    g_ref[...] = ((g_ref[...] - target) * mask / count).astype(BF).astype(F32)

    def backward(i, carry):
        l = L - 1 - i
        g = g_ref[...]
        gb = g.astype(BF)
        pay_ref[l, 0:T, :] = gb
        act = act_ref[l].astype(F32)
        share = jnp.where(core == 0, act[:, 0:H], act[:, H:])
        pay_ref[l, T:T + T // 2, 0:H] = share[0:T // 2].astype(BF)
        pay_ref[l, T:T + T // 2, H:] = share[T // 2:].astype(BF)
        grad_act = lax.dot_general(
            gb, w_ref[l], (((1,), (1,)), ((), ())), preferred_element_type=F32)
        grad_conv = grad_act * slope_ref[l]
        gpad_ref[8:T + 8, :] = grad_conv
        taps = taps_ref[l, 0:KER, :]
        rows = []
        for k in range(KER):
            rows.append(jnp.sum(grad_conv * norm_ref[l, 6 + k:T + 6 + k, :], axis=0, keepdims=True))
        total = jnp.concatenate(rows, axis=0)
        hi = total.astype(BF).astype(F32)
        packed = jnp.concatenate([hi, total - hi, jnp.zeros((TAPS - 2 * KER, D), F32)], axis=0)
        pay_ref[l, T + T // 2:, :] = packed.astype(BF)
        grad_norm = taps[0:1] * gpad_ref[10:T + 10, :]
        for k in range(1, KER):
            grad_norm = grad_norm + taps[k:k + 1] * gpad_ref[10 - k:T + 10 - k, :]
        grad_norm = grad_norm * mask
        vals = vals_ref[l]
        inv = inv_ref[l][:, 0:1]
        mean = jnp.mean(grad_norm * vals, axis=-1, keepdims=True)
        g_ref[...] = (g + (inv * grad_norm - vals * (inv * inv * inv * mean))).astype(BF).astype(F32)
        return carry

    lax.fori_loop(0, L, backward, 0)


def grad_kernel(recv_ref, out_ref, act_ref, flat_ref, row_ref, chunk_ref):
    half = T // 2
    for i in range(L):
        act_ref[i * T:i * T + half, :] = recv_ref[i, T:T + half, 0:H]
        act_ref[i * T + half:(i + 1) * T, :] = recv_ref[i, T:T + half, H:]
    g = recv_ref[:, 0:T, :].reshape(L * T, D)
    grad = lax.dot_general(
        act_ref[...], g, (((0,), (0,)), ((), ())), preferred_element_type=F32)
    for b in range(D // 128):
        flat_ref[b * H:(b + 1) * H, :] = grad[:, b * 128:(b + 1) * 128]
    taps = recv_ref[0, T + half:, :].astype(F32)
    for i in range(1, L):
        taps = taps + recv_ref[i, T + half:, :].astype(F32)
    total = taps[0:KER] + taps[KER:2 * KER]
    hi = total.astype(BF).astype(F32)
    low = total - hi
    chunk_ref[CHUNK:, :] = jnp.zeros((CROWS - CHUNK, 128), F32)
    for j in range(PEERS):
        chunk_ref[0:CHUNK, :] = flat_ref[j * CHUNK:(j + 1) * CHUNK, :]
        if j < KER * 6:
            k, b = divmod(j, 6)
            chunk_ref[CHUNK:CHUNK + 1, :] = hi[k:k + 1, b * 128:(b + 1) * 128]
            chunk_ref[CHUNK + 1:CHUNK + 2, :] = low[k:k + 1, b * 128:(b + 1) * 128]
        out_ref[j] = chunk_ref[...].astype(BF)


def sum_kernel(parts_ref, out_ref, chunk_ref):
    total = parts_ref[0].astype(F32)
    for j in range(1, PEERS):
        total = total + parts_ref[j].astype(F32)
    chunk_ref[...] = total
    tap = total[CHUNK:CHUNK + 1] + total[CHUNK + 1:CHUNK + 2]
    hi = tap.astype(BF).astype(F32)
    chunk_ref[CHUNK:CHUNK + 1, :] = hi
    chunk_ref[CHUNK + 1:CHUNK + 2, :] = tap - hi
    mine = chunk_ref[...].astype(BF)
    for j in range(PEERS):
        out_ref[j] = mine


def place_kernel(mine_ref, theirs_ref, grad_ref, taps_ref, flat_ref):
    core = lax.axis_index("c")
    for ref, which in ((mine_ref, core), (theirs_ref, 1 - core)):
        start = pl.multiple_of(which * H, H)
        for j in range(PEERS):
            flat_ref[j * CHUNK:(j + 1) * CHUNK, :] = ref[j, 0:CHUNK, :].astype(F32)
        for b in range(D // 128):
            grad_ref[0, pl.ds(start, H), b * 128:(b + 1) * 128] = (
                flat_ref[b * H:(b + 1) * H, :].astype(BF))
    for j in range(KER * 6):
        k, b = divmod(j, 6)
        pair = mine_ref[j, CHUNK:, :].astype(F32)
        taps_ref[k, :, b * 128:(b + 1) * 128] = pair[0:1] + pair[1:2]


def params(mib):
    return pltpu.CompilerParams(vmem_limit_bytes=mib * MIB)


def body(features, lengths, front_weight, pointwise, kernel, targets):
    ring = route((2, 4), lambda c, x: (c, (x + 1 if c == 0 else x - 1) % 4))
    pair = route(
        (4, 2, 2),
        lambda h, c, z: (h, c, 1 - z) if c == 0 else ((h + 2 * z - 1) % 4, c, 1 - z),
    )

    def along_x(a):
        return lax.ppermute(a, ("c", "x"), ring)

    def along_z(a):
        return lax.ppermute(a, ("zh", "c", "zl"), pair)

    def to_core(a):
        return lax.ppermute(a, "c", [(0, 1), (1, 0)])

    both, near, io = pl.pallas_call(
        prep_kernel,
        name="prep",
        out_shape=(
            jax.ShapeDtypeStruct((PIECE + H, D), BF),
            jax.ShapeDtypeStruct((PIECE, D), BF),
            jax.ShapeDtypeStruct((INROWS, FEAT + D), BF),
        ),
        in_specs=[ANY, VMEM, ANY, ANY, SMEM],
        out_specs=(ANY, ANY, ANY),
        scratch_shapes=[
            pltpu.VMEM((TAPS, D), BF),
            pltpu.VMEM((INROWS - T, FEAT + D), BF),
            pltpu.SemaphoreType.DMA((8,)),
        ],
    )(pointwise, jnp.transpose(kernel, (1, 0, 2)), features, targets, lengths)

    beside, n3 = lax.optimization_barrier((along_x(both), along_z(near)))
    io_other = to_core(io)
    n2 = along_x(beside[:PIECE])
    slant = along_z(beside)
    n5 = along_z(n2)
    here = [both, beside, n3, n2, slant, n5]
    there = [to_core(a) for a in (beside, n3, n2, slant, n5)]

    payload = pl.pallas_call(
        model_kernel,
        name="model",
        out_shape=jax.ShapeDtypeStruct((L, PAY, D), BF),
        in_specs=[ANY, ANY, VMEM] + [ANY] * 11,
        out_specs=VMEM,
        scratch_shapes=[
            pltpu.VMEM((L, D, D), BF),
            pltpu.VMEM((L, TAPS, D), BF),
            pltpu.VMEM((L, 8, D), F32),
            pltpu.VMEM((L, T, D), F32),
            pltpu.VMEM((L, T, 128), F32),
            pltpu.VMEM((L, T + 16, D), F32),
            pltpu.VMEM((L, T, D), F32),
            pltpu.VMEM((L, T, D), BF),
            pltpu.VMEM((T + 16, D), F32),
            pltpu.VMEM((T, D), F32),
            pltpu.VMEM((2, INROWS, FEAT + D), BF),
            pltpu.SemaphoreType.DMA((L,)),
            pltpu.SemaphoreType.DMA((L,)),
            pltpu.SemaphoreType.DMA((2,)),
        ],
        compiler_params=params(28),
    )(io, io_other, front_weight, *here, *there)

    received = lax.all_to_all(payload, ("x", "zl"), 0, 0)

    parts = pl.pallas_call(
        grad_kernel,
        name="grad",
        out_shape=jax.ShapeDtypeStruct((PEERS, CROWS, 128), BF),
        in_specs=[VMEM],
        out_specs=VMEM,
        scratch_shapes=[
            pltpu.VMEM((L * T, H), BF),
            pltpu.VMEM((H * 6, 128), F32),
            pltpu.VMEM((8, D), F32),
            pltpu.VMEM((CROWS, 128), F32),
        ],
        compiler_params=params(24),
    )(received)

    scattered = lax.all_to_all(parts, ("y", "zh"), 0, 0)

    mine = pl.pallas_call(
        sum_kernel,
        name="total",
        out_shape=jax.ShapeDtypeStruct((PEERS, CROWS, 128), BF),
        in_specs=[VMEM],
        out_specs=VMEM,
        scratch_shapes=[pltpu.VMEM((CROWS, 128), F32)],
        compiler_params=params(16),
    )(scattered)

    half = lax.all_to_all(mine, ("y", "zh"), 0, 0)
    other_half = to_core(half)

    grads, tap_grads = pl.pallas_call(
        place_kernel,
        name="place",
        out_shape=(
            jax.ShapeDtypeStruct((1, D, D), BF),
            jax.ShapeDtypeStruct((KER, 1, D), F32),
        ),
        in_specs=[VMEM, VMEM],
        out_specs=(VMEM, VMEM),
        scratch_shapes=[pltpu.VMEM((H * 6, 128), F32)],
        compiler_params=params(16),
    )(half, other_half)
    return grads, jnp.transpose(tap_grads, (1, 0, 2))


def solution(mesh):
    fine = Mesh(mesh.devices.reshape(8, 4, 2, 4, 2), ("y", "zh", "c", "x", "zl"))
    dp = ("y", "zh", "c")
    section = ("x", "zl")
    return jax.shard_map(
        body,
        mesh=fine,
        in_specs=(
            P(dp, None, None),
            P(dp),
            P(),
            P(section, None, None),
            P(section, None, None),
            P(dp, None, None),
        ),
        out_specs=(P(section, None, None), P(section, None, None)),
        check_vma=False,
    )
```

```python
import itertools

import jax
import jax.numpy as jnp
from jax import lax
from jax.experimental import pallas as pl
from jax.experimental.pallas import tpu as pltpu
from jax.sharding import Mesh, PartitionSpec as P

EPS = 1e-06
BF = jnp.bfloat16
F32 = jnp.float32

D = 768
H = 384
KER = 5
FEAT = 512
T = 64
L = 8
TAPS = 16
INROWS = T + 16
HT = T // 2
PAY = T + HT + TAPS
PEERS = 32
CHUNK = 72
CROWS = 80
MIB = 1024 * 1024

VMEM = pl.BlockSpec(memory_space=pltpu.VMEM)
ANY = pl.BlockSpec(memory_space=pl.ANY)
SMEM = pl.BlockSpec(memory_space=pltpu.SMEM)


def route(shape, step):
    spots = list(itertools.product(*map(range, shape)))
    place = {spot: i for i, spot in enumerate(spots)}
    return [(place[spot], place[step(*spot)]) for spot in spots]


def split3(x):
    hi = x.astype(BF).astype(F32)
    rest = x - hi
    mid = rest.astype(BF).astype(F32)
    return hi, mid, rest - mid


def where_am_i():
    section = 2 * lax.axis_index("x") + lax.axis_index("zl")
    return section, lax.axis_index("c")


def prep_kernel(taps_ref, feat_ref, targ_ref, len_ref, packed_ref, io_ref):
    section, _ = where_am_i()
    utt = lax.rem(section, 4)
    taps = jnp.concatenate([taps_ref[k] for k in range(KER)], axis=0)
    hi, mid, low = split3(taps)
    packed = jnp.concatenate([hi, mid, low, jnp.zeros((1, D), F32)], axis=0).astype(BF)
    for i in range(L):
        packed_ref[i] = packed
    io_ref[0:T, 0:FEAT] = feat_ref[utt]
    io_ref[0:T, FEAT:] = targ_ref[utt]
    count = len_ref[utt].astype(F32)
    io_ref[T:, :] = jnp.full((INROWS - T, FEAT + D), count, F32).astype(BF)


def fold(x):
    return jnp.concatenate([x[0:HT], x[HT:]], axis=1)


def model_kernel(
    io_a_ref, io_b_ref, front_ref, traw_ref,
    own_w, near_w, flip_w, n2, slant_w, n5, anti_w, m2, far_w, m5,
    pay_ref,
    w_ref, taps_ref, vals_ref, inv_ref, norm_ref, slope_ref, act_ref, gpad_ref, g_ref,
    io_ref, wsem, isem,
):
    section, core = where_am_i()
    col = lax.div(section, 2)
    row = lax.rem(section, 2)
    other = 1 - core
    side = lax.rem(col + 3 + 2 * core, 4)
    anti = lax.rem(col + 1 + 2 * core, 4)
    across = lax.rem(col + 2, 4)
    flip = 1 - row
    inputs = [
        pltpu.make_async_copy(ref, io_ref.at[i], isem.at[i])
        for i, ref in enumerate((io_a_ref, io_b_ref))
    ]
    for copy in inputs:
        copy.start()

    for piece, c, r in (
        (own_w, col, row), (near_w, side, row), (flip_w, col, flip), (slant_w, side, flip),
        (anti_w, anti, row), (far_w, anti, flip),
    ):
        layer = 2 * c + r
        pltpu.make_async_copy(piece, w_ref.at[layer], wsem.at[layer]).start()
    for piece, c, r, part in (
        (n2, across, row, core), (m2, across, row, other),
        (n5, across, flip, core), (m5, across, flip, other),
    ):
        layer = 2 * c + r
        start = pl.multiple_of(part * H, H)
        pltpu.make_async_copy(piece, w_ref.at[layer, pl.ds(start, H)], wsem.at[layer]).start()

    for copy in inputs:
        copy.wait()
    own = core == lax.div(section, 4)
    pick = jnp.where(own, 1.0, 0.0).astype(F32)
    io = io_ref[0].astype(F32) * pick + io_ref[1].astype(F32) * (1.0 - pick)
    count = io[T:T + 1, 0:1]
    target = io[0:T, FEAT:]
    frame = lax.broadcasted_iota(jnp.int32, (T, 1), 0).astype(F32)
    mask = jnp.where(frame < count, 1.0, 0.0).astype(F32)
    hidden = jnp.dot(io[0:T, 0:FEAT].astype(BF), front_ref[...], preferred_element_type=F32)
    g_ref[...] = hidden.astype(BF).astype(F32)

    edge = jnp.zeros((8, D), F32)
    gpad_ref[0:8, :] = edge
    gpad_ref[T + 8:, :] = edge

    def forward(l, carry):
        pltpu.make_async_copy(w_ref.at[l], w_ref.at[l], wsem.at[l]).wait()
        raw = traw_ref[l].astype(F32)
        taps = raw[0:KER] + raw[KER:2 * KER] + raw[2 * KER:3 * KER]
        taps_ref[l, 0:KER, :] = taps
        vals = g_ref[...]
        inv = lax.rsqrt(jnp.mean(vals * vals, axis=-1, keepdims=True) + EPS)
        norm = vals * inv * mask
        vals_ref[l] = vals
        inv_ref[l] = jnp.broadcast_to(inv, (T, 128))
        norm_ref[l, 0:8, :] = edge
        norm_ref[l, T + 8:, :] = edge
        norm_ref[l, 8:T + 8, :] = norm
        conv = taps[0:1] * norm_ref[l, 6:T + 6, :]
        for k in range(1, KER):
            conv = conv + taps[k:k + 1] * norm_ref[l, 6 + k:T + 6 + k, :]
        sig = jax.nn.sigmoid(conv)
        act = (conv * sig).astype(BF)
        slope_ref[l] = sig * (1.0 + conv * (1.0 - sig))
        act_ref[l] = act
        out = vals + jnp.dot(act, w_ref[l], preferred_element_type=F32)
        g_ref[...] = out.astype(BF).astype(F32)
        return carry

    lax.fori_loop(0, L, forward, 0)

    g_ref[...] = ((g_ref[...] - target) * mask / count).astype(BF).astype(F32)

    def backward(i, carry):
        l = L - 1 - i
        g = g_ref[...]
        gb = g.astype(BF)
        pay_ref[l, 0:T, :] = gb
        act = act_ref[l].astype(F32)
        share = jnp.where(core == 0, act[:, 0:H], act[:, H:])
        pay_ref[l, T:T + HT, :] = fold(share).astype(BF)
        grad_act = lax.dot_general(
            gb, w_ref[l], (((1,), (1,)), ((), ())), preferred_element_type=F32)
        grad_conv = grad_act * slope_ref[l]
        gpad_ref[8:T + 8, :] = grad_conv
        taps = taps_ref[l, 0:KER, :]
        rows = []
        for k in range(KER):
            rows.append(jnp.sum(grad_conv * norm_ref[l, 6 + k:T + 6 + k, :], axis=0, keepdims=True))
        total = jnp.concatenate(rows, axis=0)
        hi = total.astype(BF).astype(F32)
        packed = jnp.concatenate([hi, total - hi, jnp.zeros((TAPS - 2 * KER, D), F32)], axis=0)
        pay_ref[l, T + HT:, :] = packed.astype(BF)
        grad_norm = taps[0:1] * gpad_ref[10:T + 10, :]
        for k in range(1, KER):
            grad_norm = grad_norm + taps[k:k + 1] * gpad_ref[10 - k:T + 10 - k, :]
        grad_norm = grad_norm * mask
        vals = vals_ref[l]
        inv = inv_ref[l][:, 0:1]
        mean = jnp.mean(grad_norm * vals, axis=-1, keepdims=True)
        g_ref[...] = (g + (inv * grad_norm - vals * (inv * inv * inv * mean))).astype(BF).astype(F32)
        return carry

    lax.fori_loop(0, L, backward, 0)


def grad_kernel(recv_ref, out_ref, act_ref, flat_ref, row_ref, chunk_ref):
    half = T // 2
    for i in range(L):
        act_ref[i * T:i * T + half, :] = recv_ref[i, T:T + half, 0:H]
        act_ref[i * T + half:(i + 1) * T, :] = recv_ref[i, T:T + half, H:]
    g = recv_ref[:, 0:T, :].reshape(L * T, D)
    grad = lax.dot_general(
        act_ref[...], g, (((0,), (0,)), ((), ())), preferred_element_type=F32)
    for b in range(D // 128):
        flat_ref[b * H:(b + 1) * H, :] = grad[:, b * 128:(b + 1) * 128]
    taps = recv_ref[0, T + half:, :].astype(F32)
    for i in range(1, L):
        taps = taps + recv_ref[i, T + half:, :].astype(F32)
    total = taps[0:KER] + taps[KER:2 * KER]
    hi = total.astype(BF).astype(F32)
    low = total - hi
    chunk_ref[CHUNK:, :] = jnp.zeros((CROWS - CHUNK, 128), F32)
    for j in range(PEERS):
        chunk_ref[0:CHUNK, :] = flat_ref[j * CHUNK:(j + 1) * CHUNK, :]
        if j < KER * 6:
            k, b = divmod(j, 6)
            chunk_ref[CHUNK:CHUNK + 1, :] = hi[k:k + 1, b * 128:(b + 1) * 128]
            chunk_ref[CHUNK + 1:CHUNK + 2, :] = low[k:k + 1, b * 128:(b + 1) * 128]
        out_ref[j] = chunk_ref[...].astype(BF)


def sum_kernel(parts_ref, out_ref, chunk_ref):
    total = parts_ref[0].astype(F32)
    for j in range(1, PEERS):
        total = total + parts_ref[j].astype(F32)
    chunk_ref[...] = total
    tap = total[CHUNK:CHUNK + 1] + total[CHUNK + 1:CHUNK + 2]
    hi = tap.astype(BF).astype(F32)
    chunk_ref[CHUNK:CHUNK + 1, :] = hi
    chunk_ref[CHUNK + 1:CHUNK + 2, :] = tap - hi
    mine = chunk_ref[...].astype(BF)
    for j in range(PEERS):
        out_ref[j] = mine


def place_kernel(mine_ref, theirs_ref, grad_ref, taps_ref, flat_ref):
    core = lax.axis_index("c")
    for ref, which in ((mine_ref, core), (theirs_ref, 1 - core)):
        start = pl.multiple_of(which * H, H)
        for j in range(PEERS):
            flat_ref[j * CHUNK:(j + 1) * CHUNK, :] = ref[j, 0:CHUNK, :].astype(F32)
        for b in range(D // 128):
            grad_ref[0, pl.ds(start, H), b * 128:(b + 1) * 128] = (
                flat_ref[b * H:(b + 1) * H, :].astype(BF))
    for j in range(KER * 6):
        k, b = divmod(j, 6)
        pair = mine_ref[j, CHUNK:, :].astype(F32)
        taps_ref[k, :, b * 128:(b + 1) * 128] = pair[0:1] + pair[1:2]


def params(mib):
    return pltpu.CompilerParams(vmem_limit_bytes=mib * MIB)


def body(features, lengths, front_weight, pointwise, kernel, targets):
    ring = route((2, 4), lambda c, x: (c, (x + 1 if c == 0 else x - 1) % 4))
    pair = route(
        (4, 2, 2),
        lambda h, c, z: (h, c, 1 - z) if c == 0 else ((h + 2 * z - 1) % 4, c, 1 - z),
    )

    def along_x(a):
        return lax.ppermute(a, ("c", "x"), ring)

    def along_z(a):
        return lax.ppermute(a, ("zh", "c", "zl"), pair)

    def to_core(a):
        return lax.ppermute(a, "c", [(0, 1), (1, 0)])

    weight = pointwise[0]
    packed, io = pl.pallas_call(
        prep_kernel,
        name="prep",
        out_shape=(
            jax.ShapeDtypeStruct((L, TAPS, D), BF),
            jax.ShapeDtypeStruct((INROWS, FEAT + D), BF),
        ),
        in_specs=[VMEM, VMEM, VMEM, SMEM],
        out_specs=(VMEM, VMEM),
    )(jnp.transpose(kernel, (1, 0, 2)), features, targets, lengths)

    beside, flipped, taps, io_other = lax.optimization_barrier((
        along_x(weight), along_z(weight),
        lax.all_to_all(packed, ("x", "zl"), 0, 0), to_core(io),
    ))
    start = lax.axis_index("c") * H
    n2 = along_x(lax.dynamic_slice_in_dim(beside, start, H, 0))
    slant = along_z(beside)
    anti = to_core(beside)
    n2, anti = lax.optimization_barrier((n2, anti))
    n5 = along_z(n2)
    here = [weight, beside, flipped, n2, slant, n5]
    there = [anti] + [to_core(a) for a in (n2, slant, n5)]

    payload = pl.pallas_call(
        model_kernel,
        name="model",
        out_shape=jax.ShapeDtypeStruct((L, PAY, D), BF),
        in_specs=[ANY, ANY, VMEM, VMEM] + [ANY] * 10,
        out_specs=VMEM,
        scratch_shapes=[
            pltpu.VMEM((L, D, D), BF),
            pltpu.VMEM((L, 8, D), F32),
            pltpu.VMEM((L, T, D), F32),
            pltpu.VMEM((L, T, 128), F32),
            pltpu.VMEM((L, T + 16, D), F32),
            pltpu.VMEM((L, T, D), F32),
            pltpu.VMEM((L, T, D), BF),
            pltpu.VMEM((T + 16, D), F32),
            pltpu.VMEM((T, D), F32),
            pltpu.VMEM((2, INROWS, FEAT + D), BF),
            pltpu.SemaphoreType.DMA((L,)),
            pltpu.SemaphoreType.DMA((2,)),
        ],
        compiler_params=params(28),
    )(io, io_other, front_weight, taps, *here, *there)

    received = lax.all_to_all(payload, ("x", "zl"), 0, 0)

    parts = pl.pallas_call(
        grad_kernel,
        name="grad",
        out_shape=jax.ShapeDtypeStruct((PEERS, CROWS, 128), BF),
        in_specs=[VMEM],
        out_specs=VMEM,
        scratch_shapes=[
            pltpu.VMEM((L * T, H), BF),
            pltpu.VMEM((H * 6, 128), F32),
            pltpu.VMEM((8, D), F32),
            pltpu.VMEM((CROWS, 128), F32),
        ],
        compiler_params=params(24),
    )(received)

    scattered = lax.all_to_all(parts, ("y", "zh"), 0, 0)

    mine = pl.pallas_call(
        sum_kernel,
        name="total",
        out_shape=jax.ShapeDtypeStruct((PEERS, CROWS, 128), BF),
        in_specs=[VMEM],
        out_specs=VMEM,
        scratch_shapes=[pltpu.VMEM((CROWS, 128), F32)],
        compiler_params=params(16),
    )(scattered)

    half = lax.all_to_all(mine, ("y", "zh"), 0, 0)
    other_half = to_core(half)

    grads, tap_grads = pl.pallas_call(
        place_kernel,
        name="place",
        out_shape=(
            jax.ShapeDtypeStruct((1, D, D), BF),
            jax.ShapeDtypeStruct((KER, 1, D), F32),
        ),
        in_specs=[VMEM, VMEM],
        out_specs=(VMEM, VMEM),
        scratch_shapes=[pltpu.VMEM((H * 6, 128), F32)],
        compiler_params=params(16),
    )(half, other_half)
    return grads, jnp.transpose(tap_grads, (1, 0, 2))


def solution(mesh):
    fine = Mesh(mesh.devices.reshape(8, 4, 2, 4, 2), ("y", "zh", "c", "x", "zl"))
    dp = ("y", "zh", "c")
    section = ("x", "zl")
    return jax.shard_map(
        body,
        mesh=fine,
        in_specs=(
            P(dp, None, None),
            P(dp),
            P(),
            P(section, None, None),
            P(section, None, None),
            P(dp, None, None),
        ),
        out_specs=(P(section, None, None), P(section, None, None)),
        check_vma=False,
    )
```

```python
import itertools

import jax
import jax.numpy as jnp
from jax import lax
from jax.experimental import pallas as pl
from jax.experimental.pallas import tpu as pltpu
from jax.sharding import Mesh, PartitionSpec as P

EPS = 1e-06
BF = jnp.bfloat16
F32 = jnp.float32

D = 768
H = 384
KER = 5
FEAT = 512
T = 64
L = 8
TAPS = 16
PIECE = H + TAPS
INROWS = T + 16
HT = T // 2
PAY = T + HT + 8
PEERS = 32
CHUNK = 72
CROWS = 80
MIB = 1024 * 1024

VMEM = pl.BlockSpec(memory_space=pltpu.VMEM)
ANY = pl.BlockSpec(memory_space=pl.ANY)
SMEM = pl.BlockSpec(memory_space=pltpu.SMEM)


def route(shape, step):
    spots = list(itertools.product(*map(range, shape)))
    place = {spot: i for i, spot in enumerate(spots)}
    return [(place[spot], place[step(*spot)]) for spot in spots]


def split3(x):
    hi = x.astype(BF).astype(F32)
    rest = x - hi
    mid = rest.astype(BF).astype(F32)
    return hi, mid, rest - mid


def where_am_i():
    section = 2 * lax.axis_index("x") + lax.axis_index("zl")
    return section, lax.axis_index("c")


def prep_kernel(
    w_ref, taps_ref, feat_ref, targ_ref, len_ref, both_ref, io_ref, sem
):
    section, core = where_am_i()
    utt = lax.rem(section, 4)
    mine = pl.multiple_of(core * H, H)
    theirs = pl.multiple_of((1 - core) * H, H)
    copies = [
        pltpu.make_async_copy(w_ref.at[0, pl.ds(mine, H)], both_ref.at[pl.ds(0, H)], sem.at[0]),
        pltpu.make_async_copy(w_ref.at[0, pl.ds(theirs, H)], both_ref.at[pl.ds(PIECE, H)], sem.at[1]),
        pltpu.make_async_copy(
            feat_ref.at[utt], io_ref.at[pl.ds(0, T), pl.ds(0, FEAT)], sem.at[2]),
        pltpu.make_async_copy(
            targ_ref.at[utt], io_ref.at[pl.ds(0, T), pl.ds(FEAT, D)], sem.at[3]),
    ]
    for copy in copies:
        copy.start()
    taps = jnp.concatenate([taps_ref[k] for k in range(KER)], axis=0)
    hi, mid, low = split3(taps)
    packed = jnp.concatenate([hi, mid, low, jnp.zeros((1, D), F32)], axis=0)
    both_ref[H:PIECE, :] = packed.astype(BF)
    count = len_ref[utt].astype(F32)
    io_ref[T:, :] = jnp.full((INROWS - T, FEAT + D), count, F32).astype(BF)
    for copy in copies:
        copy.wait()


def front_kernel(io_a_ref, io_b_ref, front_ref, out_ref):
    section, core = where_am_i()
    own = core == lax.div(section, 4)
    pick = jnp.where(own, 1.0, 0.0).astype(F32)
    io = io_a_ref[...].astype(F32) * pick + io_b_ref[...].astype(F32) * (1.0 - pick)
    out_ref[0:T, :] = jnp.dot(
        io[0:T, 0:FEAT].astype(BF), front_ref[...], preferred_element_type=F32).astype(BF)
    out_ref[T:, :] = io[:, FEAT:].astype(BF)


def fold(x):
    return jnp.concatenate([x[0:HT], x[HT:]], axis=1)


def model_kernel(
    start_ref,
    own_w, near_w, flip_w, n2, slant_w, n5, anti_w, m2, far_w, m5,
    pay_ref,
    w_ref, traw_ref, taps_ref, vals_ref, inv_ref, norm_ref, slope_ref, act_ref, gpad_ref, g_ref,
    wsem, tsem,
):
    section, core = where_am_i()
    col = lax.div(section, 2)
    row = lax.rem(section, 2)
    other = 1 - core
    side = lax.rem(col + 3 + 2 * core, 4)
    anti = lax.rem(col + 1 + 2 * core, 4)
    across = lax.rem(col + 2, 4)
    flip = 1 - row

    def bring(piece, first, c, r, part, with_taps):
        layer = 2 * c + r
        start = pl.multiple_of(part * H, H)
        pltpu.make_async_copy(
            piece.at[pl.ds(first, H)], w_ref.at[layer, pl.ds(start, H)], wsem.at[layer]).start()
        if with_taps:
            pltpu.make_async_copy(
                piece.at[pl.ds(H, TAPS)], traw_ref.at[layer], tsem.at[layer]).start()

    for piece, c, r, part in (
        (own_w, col, row, core), (near_w, side, row, core), (flip_w, col, flip, core),
        (slant_w, side, flip, core), (anti_w, anti, row, other), (far_w, anti, flip, other),
    ):
        bring(piece, 0, c, r, part, True)
        bring(piece, PIECE, c, r, 1 - part, False)
    for piece, mirror, r in ((n2, m2, row), (n5, m5, flip)):
        bring(piece, 0, across, r, core, True)
        bring(mirror, 0, across, r, other, False)

    count = start_ref[2 * T:, :].astype(F32)[0:1, 0:1]
    target = start_ref[T:2 * T, :].astype(F32)
    frame = lax.broadcasted_iota(jnp.int32, (T, 1), 0).astype(F32)
    mask = jnp.where(frame < count, 1.0, 0.0).astype(F32)
    g_ref[...] = start_ref[0:T, :].astype(F32)

    edge = jnp.zeros((8, D), F32)
    gpad_ref[0:8, :] = edge
    gpad_ref[T + 8:, :] = edge

    def forward(l, carry):
        pltpu.make_async_copy(traw_ref.at[l], traw_ref.at[l], tsem.at[l]).wait()
        pltpu.make_async_copy(w_ref.at[l], w_ref.at[l], wsem.at[l]).wait()
        raw = traw_ref[l].astype(F32)
        taps = raw[0:KER] + raw[KER:2 * KER] + raw[2 * KER:3 * KER]
        taps_ref[l, 0:KER, :] = taps
        vals = g_ref[...]
        inv = lax.rsqrt(jnp.mean(vals * vals, axis=-1, keepdims=True) + EPS)
        norm = vals * inv * mask
        vals_ref[l] = vals
        inv_ref[l] = jnp.broadcast_to(inv, (T, 128))
        norm_ref[l, 0:8, :] = edge
        norm_ref[l, T + 8:, :] = edge
        norm_ref[l, 8:T + 8, :] = norm
        conv = taps[0:1] * norm_ref[l, 6:T + 6, :]
        for k in range(1, KER):
            conv = conv + taps[k:k + 1] * norm_ref[l, 6 + k:T + 6 + k, :]
        sig = jax.nn.sigmoid(conv)
        act = (conv * sig).astype(BF)
        slope_ref[l] = sig * (1.0 + conv * (1.0 - sig))
        act_ref[l] = act
        out = vals + jnp.dot(act, w_ref[l], preferred_element_type=F32)
        g_ref[...] = out.astype(BF).astype(F32)
        return carry

    lax.fori_loop(0, L, forward, 0)

    g_ref[...] = ((g_ref[...] - target) * mask / count).astype(BF).astype(F32)

    def backward(i, carry):
        l = L - 1 - i
        g = g_ref[...]
        gb = g.astype(BF)
        pay_ref[l, 0:T, :] = gb
        act = act_ref[l].astype(F32)
        share = jnp.where(core == 0, act[:, 0:H], act[:, H:])
        pay_ref[l, T:T + HT, :] = fold(share).astype(BF)
        grad_act = lax.dot_general(
            gb, w_ref[l], (((1,), (1,)), ((), ())), preferred_element_type=F32)
        grad_conv = grad_act * slope_ref[l]
        gpad_ref[8:T + 8, :] = grad_conv
        taps = taps_ref[l, 0:KER, :]
        rows = []
        for k in range(KER):
            rows.append(jnp.sum(grad_conv * norm_ref[l, 6 + k:T + 6 + k, :], axis=0, keepdims=True))
        total = jnp.concatenate(rows, axis=0)
        hi = total.astype(BF).astype(F32)
        part = jnp.where(core == 0, hi, total - hi)
        packed = jnp.concatenate([part, jnp.zeros((8 - KER, D), F32)], axis=0)
        pay_ref[l, T + HT:, :] = packed.astype(BF)
        grad_norm = taps[0:1] * gpad_ref[10:T + 10, :]
        for k in range(1, KER):
            grad_norm = grad_norm + taps[k:k + 1] * gpad_ref[10 - k:T + 10 - k, :]
        grad_norm = grad_norm * mask
        vals = vals_ref[l]
        inv = inv_ref[l][:, 0:1]
        mean = jnp.mean(grad_norm * vals, axis=-1, keepdims=True)
        g_ref[...] = (g + (inv * grad_norm - vals * (inv * inv * inv * mean))).astype(BF).astype(F32)
        return carry

    lax.fori_loop(0, L, backward, 0)


def grad_kernel(recv_ref, out_ref, act_ref, flat_ref, row_ref, chunk_ref):
    half = T // 2
    for i in range(L):
        act_ref[i * T:i * T + half, :] = recv_ref[i, T:T + half, 0:H]
        act_ref[i * T + half:(i + 1) * T, :] = recv_ref[i, T:T + half, H:]
    g = recv_ref[:, 0:T, :].reshape(L * T, D)
    grad = lax.dot_general(
        act_ref[...], g, (((0,), (0,)), ((), ())), preferred_element_type=F32)
    for b in range(D // 128):
        flat_ref[b * H:(b + 1) * H, :] = grad[:, b * 128:(b + 1) * 128]
    taps = recv_ref[0, T + half:, :].astype(F32)
    for i in range(1, L):
        taps = taps + recv_ref[i, T + half:, :].astype(F32)
    total = taps[0:KER]
    hi = total.astype(BF).astype(F32)
    low = total - hi
    chunk_ref[CHUNK:, :] = jnp.zeros((CROWS - CHUNK, 128), F32)
    for j in range(PEERS):
        chunk_ref[0:CHUNK, :] = flat_ref[j * CHUNK:(j + 1) * CHUNK, :]
        if j < KER * 6:
            k, b = divmod(j, 6)
            chunk_ref[CHUNK:CHUNK + 1, :] = hi[k:k + 1, b * 128:(b + 1) * 128]
            chunk_ref[CHUNK + 1:CHUNK + 2, :] = low[k:k + 1, b * 128:(b + 1) * 128]
        out_ref[j] = chunk_ref[...].astype(BF)


def sum_kernel(parts_ref, out_ref, chunk_ref):
    total = parts_ref[0].astype(F32)
    for j in range(1, PEERS):
        total = total + parts_ref[j].astype(F32)
    chunk_ref[...] = total
    tap = total[CHUNK:CHUNK + 1] + total[CHUNK + 1:CHUNK + 2]
    hi = tap.astype(BF).astype(F32)
    chunk_ref[CHUNK:CHUNK + 1, :] = hi
    chunk_ref[CHUNK + 1:CHUNK + 2, :] = tap - hi
    mine = chunk_ref[...].astype(BF)
    for j in range(PEERS):
        out_ref[j] = mine


def place_kernel(mine_ref, theirs_ref, grad_ref, taps_ref, flat_ref):
    core = lax.axis_index("c")
    for ref, which in ((mine_ref, core), (theirs_ref, 1 - core)):
        start = pl.multiple_of(which * H, H)
        for j in range(PEERS):
            flat_ref[j * CHUNK:(j + 1) * CHUNK, :] = ref[j, 0:CHUNK, :].astype(F32)
        for b in range(D // 128):
            grad_ref[0, pl.ds(start, H), b * 128:(b + 1) * 128] = (
                flat_ref[b * H:(b + 1) * H, :].astype(BF))
    for j in range(KER * 6):
        k, b = divmod(j, 6)
        pair = mine_ref[j, CHUNK:, :].astype(F32) + theirs_ref[j, CHUNK:, :].astype(F32)
        taps_ref[k, :, b * 128:(b + 1) * 128] = pair[0:1] + pair[1:2]


def params(mib):
    return pltpu.CompilerParams(vmem_limit_bytes=mib * MIB)


def body(features, lengths, front_weight, pointwise, kernel, targets):
    ring = route((2, 4), lambda c, x: (c, (x + 1 if c == 0 else x - 1) % 4))
    pair = route(
        (4, 2, 2),
        lambda h, c, z: (h, c, 1 - z) if c == 0 else ((h + 2 * z - 1) % 4, c, 1 - z),
    )

    def along_x(a):
        return lax.ppermute(a, ("c", "x"), ring)

    def along_z(a):
        return lax.ppermute(a, ("zh", "c", "zl"), pair)

    def to_core(a):
        return lax.ppermute(a, "c", [(0, 1), (1, 0)])

    both, io = pl.pallas_call(
        prep_kernel,
        name="prep",
        out_shape=(
            jax.ShapeDtypeStruct((PIECE + H, D), BF),
            jax.ShapeDtypeStruct((INROWS, FEAT + D), BF),
        ),
        in_specs=[ANY, VMEM, ANY, ANY, SMEM],
        out_specs=(VMEM, VMEM),
        scratch_shapes=[pltpu.SemaphoreType.DMA((4,))],
    )(pointwise, jnp.transpose(kernel, (1, 0, 2)), features, targets, lengths)

    begin = pl.pallas_call(
        front_kernel,
        name="front",
        out_shape=jax.ShapeDtypeStruct((2 * T + INROWS - T, D), BF),
        in_specs=[VMEM, VMEM, VMEM],
        out_specs=VMEM,
    )(io, to_core(io), front_weight)
    beside, flipped, begin = lax.optimization_barrier((along_x(both), along_z(both), begin))
    n2 = along_x(beside[:PIECE])
    slant = along_z(beside)
    n5 = along_z(n2)
    here = [both, beside, flipped, n2, slant, n5]
    there = [to_core(a) for a in (beside, n2, slant, n5)]

    payload = pl.pallas_call(
        model_kernel,
        name="model",
        out_shape=jax.ShapeDtypeStruct((L, PAY, D), BF),
        in_specs=[VMEM] + [ANY] * 10,
        out_specs=VMEM,
        scratch_shapes=[
            pltpu.VMEM((L, D, D), BF),
            pltpu.VMEM((L, TAPS, D), BF),
            pltpu.VMEM((L, 8, D), F32),
            pltpu.VMEM((L, T, D), F32),
            pltpu.VMEM((L, T, 128), F32),
            pltpu.VMEM((L, T + 16, D), F32),
            pltpu.VMEM((L, T, D), F32),
            pltpu.VMEM((L, T, D), BF),
            pltpu.VMEM((T + 16, D), F32),
            pltpu.VMEM((T, D), F32),
            pltpu.SemaphoreType.DMA((L,)),
            pltpu.SemaphoreType.DMA((L,)),
        ],
        compiler_params=params(28),
    )(begin, *here, *there)

    received = lax.all_to_all(payload, ("x", "zl"), 0, 0)

    parts = pl.pallas_call(
        grad_kernel,
        name="grad",
        out_shape=jax.ShapeDtypeStruct((PEERS, CROWS, 128), BF),
        in_specs=[VMEM],
        out_specs=VMEM,
        scratch_shapes=[
            pltpu.VMEM((L * T, H), BF),
            pltpu.VMEM((H * 6, 128), F32),
            pltpu.VMEM((8, D), F32),
            pltpu.VMEM((CROWS, 128), F32),
        ],
        compiler_params=params(24),
    )(received)

    scattered = lax.all_to_all(parts, ("y", "zh"), 0, 0)

    mine = pl.pallas_call(
        sum_kernel,
        name="total",
        out_shape=jax.ShapeDtypeStruct((PEERS, CROWS, 128), BF),
        in_specs=[VMEM],
        out_specs=VMEM,
        scratch_shapes=[pltpu.VMEM((CROWS, 128), F32)],
        compiler_params=params(16),
    )(scattered)

    half = lax.all_to_all(mine, ("y", "zh"), 0, 0)
    other_half = to_core(half)

    grads, tap_grads = pl.pallas_call(
        place_kernel,
        name="place",
        out_shape=(
            jax.ShapeDtypeStruct((1, D, D), BF),
            jax.ShapeDtypeStruct((KER, 1, D), F32),
        ),
        in_specs=[VMEM, VMEM],
        out_specs=(VMEM, VMEM),
        scratch_shapes=[pltpu.VMEM((H * 6, 128), F32)],
        compiler_params=params(16),
    )(half, other_half)
    return grads, jnp.transpose(tap_grads, (1, 0, 2))


def solution(mesh):
    fine = Mesh(mesh.devices.reshape(8, 4, 2, 4, 2), ("y", "zh", "c", "x", "zl"))
    dp = ("y", "zh", "c")
    section = ("x", "zl")
    return jax.shard_map(
        body,
        mesh=fine,
        in_specs=(
            P(dp, None, None),
            P(dp),
            P(),
            P(section, None, None),
            P(section, None, None),
            P(dp, None, None),
        ),
        out_specs=(P(section, None, None), P(section, None, None)),
        check_vma=False,
    )
```

```python
import itertools

import jax
import jax.numpy as jnp
from jax import lax
from jax.experimental import pallas as pl
from jax.experimental.pallas import tpu as pltpu
from jax.sharding import Mesh, PartitionSpec as P

EPS = 1e-06
BF = jnp.bfloat16
F32 = jnp.float32

D = 768
H = 384
KER = 5
FEAT = 512
T = 64
L = 8
TAPS = 16
NEAR = H + TAPS
FAR = H + 2 * TAPS
INROWS = T + 16
HT = T // 2
PAY = T + HT + 8
PEERS = 32
CHUNK = 72
CROWS = 80
MIB = 1024 * 1024

VMEM = pl.BlockSpec(memory_space=pltpu.VMEM)
ANY = pl.BlockSpec(memory_space=pl.ANY)
SMEM = pl.BlockSpec(memory_space=pltpu.SMEM)


def route(shape, step):
    spots = list(itertools.product(*map(range, shape)))
    place = {spot: i for i, spot in enumerate(spots)}
    return [(place[spot], place[step(*spot)]) for spot in spots]


def split3(x):
    hi = x.astype(BF).astype(F32)
    rest = x - hi
    mid = rest.astype(BF).astype(F32)
    return hi, mid, rest - mid


def where_am_i():
    section = 2 * lax.axis_index("x") + lax.axis_index("zl")
    return section, lax.axis_index("c")


def prep_kernel(w_ref, taps_ref, feat_ref, targ_ref, len_ref, near_ref, far_ref, io_ref, sem):
    section, core = where_am_i()
    utt = lax.rem(section, 4)
    mine = pl.multiple_of(core * H, H)
    theirs = pl.multiple_of((1 - core) * H, H)
    copies = [
        pltpu.make_async_copy(w_ref.at[0, pl.ds(mine, H)], near_ref.at[pl.ds(0, H)], sem.at[0]),
        pltpu.make_async_copy(w_ref.at[0, pl.ds(theirs, H)], far_ref.at[pl.ds(0, H)], sem.at[1]),
        pltpu.make_async_copy(
            feat_ref.at[utt], io_ref.at[pl.ds(0, T), pl.ds(0, FEAT)], sem.at[2]),
        pltpu.make_async_copy(
            targ_ref.at[utt], io_ref.at[pl.ds(0, T), pl.ds(FEAT, D)], sem.at[3]),
    ]
    for copy in copies:
        copy.start()
    taps = jnp.concatenate([taps_ref[k] for k in range(KER)], axis=0)
    hi, mid, low = split3(taps)
    packed = jnp.concatenate([hi, mid, low, jnp.zeros((1, D), F32)], axis=0).astype(BF)
    near_ref[H:, :] = packed
    far_ref[H:NEAR, :] = packed
    far_ref[NEAR:, :] = packed
    count = len_ref[utt].astype(F32)
    io_ref[T:, :] = jnp.full((INROWS - T, FEAT + D), count, F32).astype(BF)
    for copy in copies:
        copy.wait()


def front_kernel(io_a_ref, io_b_ref, front_ref, out_ref):
    section, core = where_am_i()
    own = core == lax.div(section, 4)
    pick = jnp.where(own, 1.0, 0.0).astype(F32)
    io = io_a_ref[...].astype(F32) * pick + io_b_ref[...].astype(F32) * (1.0 - pick)
    out_ref[0:T, :] = jnp.dot(
        io[0:T, 0:FEAT].astype(BF), front_ref[...], preferred_element_type=F32).astype(BF)
    out_ref[T:, :] = io[:, FEAT:].astype(BF)


def fold(x):
    return jnp.concatenate([x[0:HT], x[HT:]], axis=1)


def model_kernel(
    start_ref,
    n0, f0, n1, f1, n2, n3, n4, f4, n5, m1, g1, m2, m3, m4, g4, m5,
    pay_ref,
    w_ref, traw_ref, taps_ref, vals_ref, inv_ref, norm_ref, slope_ref, act_ref, gpad_ref, g_ref,
    wsem, tsem,
):
    section, core = where_am_i()
    col = lax.div(section, 2)
    row = lax.rem(section, 2)
    other = 1 - core
    side = lax.rem(col + 3 + 2 * core, 4)
    anti = lax.rem(col + 1 + 2 * core, 4)
    across = lax.rem(col + 2, 4)
    flip = 1 - row

    def bring(piece, c, r, part, with_taps):
        layer = 2 * c + r
        start = pl.multiple_of(part * H, H)
        pltpu.make_async_copy(
            piece.at[pl.ds(0, H)], w_ref.at[layer, pl.ds(start, H)], wsem.at[layer]).start()
        if with_taps:
            pltpu.make_async_copy(
                piece.at[pl.ds(H, TAPS)], traw_ref.at[layer], tsem.at[layer]).start()

    for near, far, c, r, part in (
        (n0, f0, col, row, core), (n1, f1, side, row, core), (n4, f4, side, flip, core),
        (m1, g1, anti, row, other), (m4, g4, anti, flip, other),
    ):
        bring(near, c, r, part, False)
        bring(far, c, r, 1 - part, True)
    for near, mirror, c, r in ((n2, m2, across, row), (n3, m3, col, flip), (n5, m5, across, flip)):
        bring(near, c, r, core, True)
        bring(mirror, c, r, other, False)

    count = start_ref[2 * T:, :].astype(F32)[0:1, 0:1]
    target = start_ref[T:2 * T, :].astype(F32)
    frame = lax.broadcasted_iota(jnp.int32, (T, 1), 0).astype(F32)
    mask = jnp.where(frame < count, 1.0, 0.0).astype(F32)
    g_ref[...] = start_ref[0:T, :].astype(F32)

    edge = jnp.zeros((8, D), F32)
    gpad_ref[0:8, :] = edge
    gpad_ref[T + 8:, :] = edge

    def forward(l, carry):
        pltpu.make_async_copy(traw_ref.at[l], traw_ref.at[l], tsem.at[l]).wait()
        pltpu.make_async_copy(w_ref.at[l], w_ref.at[l], wsem.at[l]).wait()
        raw = traw_ref[l].astype(F32)
        taps = raw[0:KER] + raw[KER:2 * KER] + raw[2 * KER:3 * KER]
        taps_ref[l, 0:KER, :] = taps
        vals = g_ref[...]
        inv = lax.rsqrt(jnp.mean(vals * vals, axis=-1, keepdims=True) + EPS)
        norm = vals * inv * mask
        vals_ref[l] = vals
        inv_ref[l] = jnp.broadcast_to(inv, (T, 128))
        norm_ref[l, 0:8, :] = edge
        norm_ref[l, T + 8:, :] = edge
        norm_ref[l, 8:T + 8, :] = norm
        conv = taps[0:1] * norm_ref[l, 6:T + 6, :]
        for k in range(1, KER):
            conv = conv + taps[k:k + 1] * norm_ref[l, 6 + k:T + 6 + k, :]
        sig = jax.nn.sigmoid(conv)
        act = (conv * sig).astype(BF)
        slope_ref[l] = sig * (1.0 + conv * (1.0 - sig))
        act_ref[l] = act
        out = vals + jnp.dot(act, w_ref[l], preferred_element_type=F32)
        g_ref[...] = out.astype(BF).astype(F32)
        return carry

    lax.fori_loop(0, L, forward, 0, unroll=True)

    g_ref[...] = ((g_ref[...] - target) * mask / count).astype(BF).astype(F32)

    def backward(i, carry):
        l = L - 1 - i
        g = g_ref[...]
        gb = g.astype(BF)
        pay_ref[l, 0:T, :] = gb
        act = act_ref[l].astype(F32)
        share = jnp.where(core == 0, act[:, 0:H], act[:, H:])
        pay_ref[l, T:T + HT, :] = fold(share).astype(BF)
        grad_act = lax.dot_general(
            gb, w_ref[l], (((1,), (1,)), ((), ())), preferred_element_type=F32)
        grad_conv = grad_act * slope_ref[l]
        gpad_ref[8:T + 8, :] = grad_conv
        taps = taps_ref[l, 0:KER, :]
        rows = []
        for k in range(KER):
            rows.append(jnp.sum(grad_conv * norm_ref[l, 6 + k:T + 6 + k, :], axis=0, keepdims=True))
        total = jnp.concatenate(rows, axis=0)
        hi = total.astype(BF).astype(F32)
        part = jnp.where(core == 0, hi, total - hi)
        packed = jnp.concatenate([part, jnp.zeros((8 - KER, D), F32)], axis=0)
        pay_ref[l, T + HT:, :] = packed.astype(BF)
        grad_norm = taps[0:1] * gpad_ref[10:T + 10, :]
        for k in range(1, KER):
            grad_norm = grad_norm + taps[k:k + 1] * gpad_ref[10 - k:T + 10 - k, :]
        grad_norm = grad_norm * mask
        vals = vals_ref[l]
        inv = inv_ref[l][:, 0:1]
        mean = jnp.mean(grad_norm * vals, axis=-1, keepdims=True)
        g_ref[...] = (g + (inv * grad_norm - vals * (inv * inv * inv * mean))).astype(BF).astype(F32)
        return carry

    lax.fori_loop(0, L, backward, 0, unroll=True)


def grad_kernel(recv_ref, out_ref, act_ref, flat_ref, row_ref, chunk_ref):
    half = T // 2
    for i in range(L):
        act_ref[i * T:i * T + half, :] = recv_ref[i, T:T + half, 0:H]
        act_ref[i * T + half:(i + 1) * T, :] = recv_ref[i, T:T + half, H:]
    g = recv_ref[:, 0:T, :].reshape(L * T, D)
    grad = lax.dot_general(
        act_ref[...], g, (((0,), (0,)), ((), ())), preferred_element_type=F32)
    for b in range(D // 128):
        flat_ref[b * H:(b + 1) * H, :] = grad[:, b * 128:(b + 1) * 128]
    taps = recv_ref[0, T + half:, :].astype(F32)
    for i in range(1, L):
        taps = taps + recv_ref[i, T + half:, :].astype(F32)
    total = taps[0:KER]
    hi = total.astype(BF).astype(F32)
    low = total - hi
    chunk_ref[CHUNK:, :] = jnp.zeros((CROWS - CHUNK, 128), F32)
    for j in range(PEERS):
        chunk_ref[0:CHUNK, :] = flat_ref[j * CHUNK:(j + 1) * CHUNK, :]
        if j < KER * 6:
            k, b = divmod(j, 6)
            chunk_ref[CHUNK:CHUNK + 1, :] = hi[k:k + 1, b * 128:(b + 1) * 128]
            chunk_ref[CHUNK + 1:CHUNK + 2, :] = low[k:k + 1, b * 128:(b + 1) * 128]
        out_ref[j] = chunk_ref[...].astype(BF)


def sum_kernel(parts_ref, out_ref, chunk_ref):
    total = parts_ref[0].astype(F32)
    for j in range(1, PEERS):
        total = total + parts_ref[j].astype(F32)
    chunk_ref[...] = total
    tap = total[CHUNK:CHUNK + 1] + total[CHUNK + 1:CHUNK + 2]
    hi = tap.astype(BF).astype(F32)
    chunk_ref[CHUNK:CHUNK + 1, :] = hi
    chunk_ref[CHUNK + 1:CHUNK + 2, :] = tap - hi
    mine = chunk_ref[...].astype(BF)
    for j in range(PEERS):
        out_ref[j] = mine


def place_kernel(mine_ref, theirs_ref, grad_ref, taps_ref, flat_ref):
    core = lax.axis_index("c")
    for ref, which in ((mine_ref, core), (theirs_ref, 1 - core)):
        start = pl.multiple_of(which * H, H)
        for j in range(PEERS):
            flat_ref[j * CHUNK:(j + 1) * CHUNK, :] = ref[j, 0:CHUNK, :].astype(F32)
        for b in range(D // 128):
            grad_ref[0, pl.ds(start, H), b * 128:(b + 1) * 128] = (
                flat_ref[b * H:(b + 1) * H, :].astype(BF))
    for j in range(KER * 6):
        k, b = divmod(j, 6)
        pair = mine_ref[j, CHUNK:, :].astype(F32) + theirs_ref[j, CHUNK:, :].astype(F32)
        taps_ref[k, :, b * 128:(b + 1) * 128] = pair[0:1] + pair[1:2]


def params(mib):
    return pltpu.CompilerParams(vmem_limit_bytes=mib * MIB)


def body(features, lengths, front_weight, pointwise, kernel, targets):
    ring = route((2, 4), lambda c, x: (c, (x + 1 if c == 0 else x - 1) % 4))
    pair = route(
        (4, 2, 2),
        lambda h, c, z: (h, c, 1 - z) if c == 0 else ((h + 2 * z - 1) % 4, c, 1 - z),
    )

    def along_x(a):
        return lax.ppermute(a, ("c", "x"), ring)

    def along_z(a):
        return lax.ppermute(a, ("zh", "c", "zl"), pair)

    def to_core(a):
        return lax.ppermute(a, "c", [(0, 1), (1, 0)])

    near, far, io = pl.pallas_call(
        prep_kernel,
        name="prep",
        out_shape=(
            jax.ShapeDtypeStruct((NEAR, D), BF),
            jax.ShapeDtypeStruct((FAR, D), BF),
            jax.ShapeDtypeStruct((INROWS, FEAT + D), BF),
        ),
        in_specs=[ANY, VMEM, ANY, ANY, SMEM],
        out_specs=(VMEM, VMEM, VMEM),
        scratch_shapes=[pltpu.SemaphoreType.DMA((4,))],
    )(pointwise, jnp.transpose(kernel, (1, 0, 2)), features, targets, lengths)
    begin = pl.pallas_call(
        front_kernel,
        name="front",
        out_shape=jax.ShapeDtypeStruct((2 * T + INROWS - T, D), BF),
        in_specs=[VMEM, VMEM, VMEM],
        out_specs=VMEM,
    )(io, to_core(io), front_weight)

    n1, n3, begin = lax.optimization_barrier((along_x(near), along_z(near), begin))
    f1 = along_x(far)
    n2 = along_x(n1)
    n4 = along_z(n1)
    f4 = along_z(f1)
    m1, m3 = to_core(n1[:H]), to_core(n3[:H])
    n2, n4, m1, m3 = lax.optimization_barrier((n2, n4, m1, m3))
    n5 = along_z(n2)
    here = [near, far, n1, f1, n2, n3, n4, f4, n5]
    there = [m1, to_core(f1), to_core(n2), m3, to_core(n4), to_core(f4), to_core(n5)]

    payload = pl.pallas_call(
        model_kernel,
        name="model",
        out_shape=jax.ShapeDtypeStruct((L, PAY, D), BF),
        in_specs=[VMEM] + [ANY] * 16,
        out_specs=VMEM,
        scratch_shapes=[
            pltpu.VMEM((L, D, D), BF),
            pltpu.VMEM((L, TAPS, D), BF),
            pltpu.VMEM((L, 8, D), F32),
            pltpu.VMEM((L, T, D), F32),
            pltpu.VMEM((L, T, 128), F32),
            pltpu.VMEM((L, T + 16, D), F32),
            pltpu.VMEM((L, T, D), F32),
            pltpu.VMEM((L, T, D), BF),
            pltpu.VMEM((T + 16, D), F32),
            pltpu.VMEM((T, D), F32),
            pltpu.SemaphoreType.DMA((L,)),
            pltpu.SemaphoreType.DMA((L,)),
        ],
        compiler_params=params(28),
    )(begin, *here, *there)

    received = lax.all_to_all(payload, ("x", "zl"), 0, 0)

    parts = pl.pallas_call(
        grad_kernel,
        name="grad",
        out_shape=jax.ShapeDtypeStruct((PEERS, CROWS, 128), BF),
        in_specs=[VMEM],
        out_specs=VMEM,
        scratch_shapes=[
            pltpu.VMEM((L * T, H), BF),
            pltpu.VMEM((H * 6, 128), F32),
            pltpu.VMEM((8, D), F32),
            pltpu.VMEM((CROWS, 128), F32),
        ],
        compiler_params=params(24),
    )(received)

    scattered = lax.all_to_all(parts, ("y", "zh"), 0, 0)

    mine = pl.pallas_call(
        sum_kernel,
        name="total",
        out_shape=jax.ShapeDtypeStruct((PEERS, CROWS, 128), BF),
        in_specs=[VMEM],
        out_specs=VMEM,
        scratch_shapes=[pltpu.VMEM((CROWS, 128), F32)],
        compiler_params=params(16),
    )(scattered)

    half = lax.all_to_all(mine, ("y", "zh"), 0, 0)
    other_half = to_core(half)

    grads, tap_grads = pl.pallas_call(
        place_kernel,
        name="place",
        out_shape=(
            jax.ShapeDtypeStruct((1, D, D), BF),
            jax.ShapeDtypeStruct((KER, 1, D), F32),
        ),
        in_specs=[VMEM, VMEM],
        out_specs=(VMEM, VMEM),
        scratch_shapes=[pltpu.VMEM((H * 6, 128), F32)],
        compiler_params=params(16),
    )(half, other_half)
    return grads, jnp.transpose(tap_grads, (1, 0, 2))


def solution(mesh):
    fine = Mesh(mesh.devices.reshape(8, 4, 2, 4, 2), ("y", "zh", "c", "x", "zl"))
    dp = ("y", "zh", "c")
    section = ("x", "zl")
    return jax.shard_map(
        body,
        mesh=fine,
        in_specs=(
            P(dp, None, None),
            P(dp),
            P(),
            P(section, None, None),
            P(section, None, None),
            P(dp, None, None),
        ),
        out_specs=(P(section, None, None), P(section, None, None)),
        check_vma=False,
    )
```

```python
import itertools

import jax
import jax.numpy as jnp
from jax import lax
from jax.experimental import pallas as pl
from jax.experimental.pallas import tpu as pltpu
from jax.sharding import Mesh, PartitionSpec as P

EPS = 1e-06
BF = jnp.bfloat16
F32 = jnp.float32

D = 768
H = 384
KER = 5
FEAT = 512
T = 64
L = 8
TAPS = 16
NEAR = H + TAPS + 8
FAR = H + 2 * TAPS
INROWS = T + 16
HT = T // 2
PAY = T + HT + 8
PEERS = 32
CHUNK = 72
CROWS = 80
MIB = 1024 * 1024

VMEM = pl.BlockSpec(memory_space=pltpu.VMEM)
ANY = pl.BlockSpec(memory_space=pl.ANY)
SMEM = pl.BlockSpec(memory_space=pltpu.SMEM)


def route(shape, step):
    spots = list(itertools.product(*map(range, shape)))
    place = {spot: i for i, spot in enumerate(spots)}
    return [(place[spot], place[step(*spot)]) for spot in spots]


def split3(x):
    hi = x.astype(BF).astype(F32)
    rest = x - hi
    mid = rest.astype(BF).astype(F32)
    return hi, mid, rest - mid


def where_am_i():
    section = 2 * lax.axis_index("x") + lax.axis_index("zl")
    return section, lax.axis_index("c")


def prep_kernel(w_ref, taps_ref, feat_ref, targ_ref, len_ref, near_ref, far_ref, io_ref, sem):
    section, core = where_am_i()
    utt = lax.rem(section, 4)
    mine = pl.multiple_of(core * H, H)
    theirs = pl.multiple_of((1 - core) * H, H)
    copies = [
        pltpu.make_async_copy(w_ref.at[0, pl.ds(mine, H)], near_ref.at[pl.ds(0, H)], sem.at[0]),
        pltpu.make_async_copy(w_ref.at[0, pl.ds(theirs, H)], far_ref.at[pl.ds(0, H)], sem.at[1]),
        pltpu.make_async_copy(
            feat_ref.at[utt], io_ref.at[pl.ds(0, T), pl.ds(0, FEAT)], sem.at[2]),
        pltpu.make_async_copy(
            targ_ref.at[utt], io_ref.at[pl.ds(0, T), pl.ds(FEAT, D)], sem.at[3]),
    ]
    for copy in copies:
        copy.start()
    taps = jnp.concatenate([taps_ref[k] for k in range(KER)], axis=0)
    hi, mid, low = split3(taps)
    packed = jnp.concatenate([hi, mid, low, jnp.zeros((1, D), F32)], axis=0).astype(BF)
    near_ref[H:H + TAPS, :] = packed
    near_ref[H + TAPS:, :] = jnp.zeros((NEAR - H - TAPS, D), BF)
    far_ref[H:H + TAPS, :] = packed
    far_ref[H + TAPS:, :] = packed
    count = len_ref[utt].astype(F32)
    io_ref[T:, :] = jnp.full((INROWS - T, FEAT + D), count, F32).astype(BF)
    for copy in copies:
        copy.wait()


def front_kernel(io_a_ref, io_b_ref, front_ref, out_ref):
    section, core = where_am_i()
    own = core == lax.div(section, 4)
    pick = jnp.where(own, 1.0, 0.0).astype(F32)
    io = io_a_ref[...].astype(F32) * pick + io_b_ref[...].astype(F32) * (1.0 - pick)
    out_ref[0:T, :] = jnp.dot(
        io[0:T, 0:FEAT].astype(BF), front_ref[...], preferred_element_type=F32).astype(BF)
    out_ref[T:, :] = io[:, FEAT:].astype(BF)


def model_kernel(
    start_ref,
    n0, f0, n1, f1, n2, n3, n4, f4, n5, m1, g1, m2, m3, m4, g4, m5,
    pay_ref,
    w_ref, traw_ref, taps_ref, inv_ref, norm_ref, slope_ref, act_ref, gpad_ref, g_ref,
    wsem, tsem,
):
    section, core = where_am_i()
    col = lax.div(section, 2)
    row = lax.rem(section, 2)
    other = 1 - core
    side = lax.rem(col + 3 + 2 * core, 4)
    anti = lax.rem(col + 1 + 2 * core, 4)
    across = lax.rem(col + 2, 4)
    flip = 1 - row

    def bring(piece, c, r, part, with_taps):
        layer = 2 * c + r
        start = pl.multiple_of(part * H, H)
        pltpu.make_async_copy(
            piece.at[pl.ds(0, H)], w_ref.at[layer, pl.ds(start, H)], wsem.at[layer]).start()
        if with_taps:
            pltpu.make_async_copy(
                piece.at[pl.ds(H, TAPS)], traw_ref.at[layer], tsem.at[layer]).start()

    for near, far, c, r, part in (
        (n0, f0, col, row, core), (n1, f1, side, row, core), (n4, f4, side, flip, core),
    ):
        bring(near, c, r, part, False)
        bring(far, c, r, 1 - part, True)
    bring(m1, anti, row, other, False)
    bring(g1, anti, row, core, True)
    bring(m4, anti, flip, other, True)
    bring(g4, anti, flip, core, False)
    for near, mirror, c, r in ((n2, m2, across, row), (n3, m3, col, flip), (n5, m5, across, flip)):
        bring(near, c, r, core, True)
        bring(mirror, c, r, other, False)

    count = start_ref[2 * T:, :].astype(F32)[0:1, 0:1]
    target = start_ref[T:2 * T, :].astype(F32)
    frame = lax.broadcasted_iota(jnp.int32, (T, 1), 0).astype(F32)
    mask = jnp.where(frame < count, 1.0, 0.0).astype(F32)
    g_ref[...] = start_ref[0:T, :].astype(F32)

    edge = jnp.zeros((8, D), F32)
    gpad_ref[0:8, :] = edge
    gpad_ref[T + 8:, :] = edge

    def forward(l, carry):
        pltpu.make_async_copy(traw_ref.at[l], traw_ref.at[l], tsem.at[l]).wait()
        pltpu.make_async_copy(w_ref.at[l], w_ref.at[l], wsem.at[l]).wait()
        raw = traw_ref[l].astype(F32)
        taps = raw[0:KER] + raw[KER:2 * KER] + raw[2 * KER:3 * KER]
        taps_ref[l, 0:KER, :] = taps
        vals = g_ref[...]
        inv = lax.rsqrt(jnp.mean(vals * vals, axis=-1, keepdims=True) + EPS)
        norm = vals * (inv * mask)
        inv_ref[l] = jnp.broadcast_to(inv, (T, 128))
        norm_ref[l, 0:8, :] = edge
        norm_ref[l, T + 8:, :] = edge
        norm_ref[l, 8:T + 8, :] = norm
        conv = taps[0:1] * norm_ref[l, 6:T + 6, :]
        for k in range(1, KER):
            conv = conv + taps[k:k + 1] * norm_ref[l, 6 + k:T + 6 + k, :]
        sig = jax.nn.sigmoid(conv)
        act = (conv * sig).astype(BF)
        slope_ref[l] = sig * (1.0 + conv * (1.0 - sig))
        act_ref[l] = act
        out = vals + jnp.dot(act, w_ref[l], preferred_element_type=F32)
        g_ref[...] = out.astype(BF).astype(F32)
        return carry

    lax.fori_loop(0, L, forward, 0, unroll=True)

    g_ref[...] = ((g_ref[...] - target) * mask / count).astype(BF).astype(F32)

    share = pl.multiple_of(core * H, H)

    def backward(i, carry):
        l = L - 1 - i
        g = g_ref[...]
        gb = g.astype(BF)
        pay_ref[l, 0:T, :] = gb
        pay_ref[l, T:T + HT, 0:H] = act_ref[l, 0:HT, pl.ds(share, H)]
        pay_ref[l, T:T + HT, H:] = act_ref[l, HT:, pl.ds(share, H)]
        grad_act = lax.dot_general(
            gb, w_ref[l], (((1,), (1,)), ((), ())), preferred_element_type=F32)
        grad_conv = grad_act * slope_ref[l]
        gpad_ref[8:T + 8, :] = grad_conv
        taps = taps_ref[l, 0:KER, :]
        rows = []
        for k in range(KER):
            rows.append(jnp.sum(grad_conv * norm_ref[l, 6 + k:T + 6 + k, :], axis=0, keepdims=True))
        total = jnp.concatenate(rows, axis=0)
        hi = total.astype(BF).astype(F32)
        part = jnp.where(core == 0, hi, total - hi)
        packed = jnp.concatenate([part, jnp.zeros((8 - KER, D), F32)], axis=0)
        pay_ref[l, T + HT:, :] = packed.astype(BF)
        grad_norm = taps[0:1] * gpad_ref[10:T + 10, :]
        for k in range(1, KER):
            grad_norm = grad_norm + taps[k:k + 1] * gpad_ref[10 - k:T + 10 - k, :]
        grad_norm = grad_norm * mask
        inv = inv_ref[l][:, 0:1]
        norm = norm_ref[l, 8:T + 8, :]
        mean = jnp.mean(grad_norm * norm, axis=-1, keepdims=True)
        g_ref[...] = (g + inv * (grad_norm - norm * mean)).astype(BF).astype(F32)
        return carry

    lax.fori_loop(0, L, backward, 0, unroll=True)


def grad_kernel(recv_ref, out_ref, act_ref, flat_ref, row_ref, chunk_ref):
    half = T // 2
    for i in range(L):
        act_ref[i * T:i * T + half, :] = recv_ref[i, T:T + half, 0:H]
        act_ref[i * T + half:(i + 1) * T, :] = recv_ref[i, T:T + half, H:]
    g = recv_ref[:, 0:T, :].reshape(L * T, D)
    grad = lax.dot_general(
        act_ref[...], g, (((0,), (0,)), ((), ())), preferred_element_type=F32)
    for b in range(D // 128):
        flat_ref[b * H:(b + 1) * H, :] = grad[:, b * 128:(b + 1) * 128]
    taps = recv_ref[0, T + half:, :].astype(F32)
    for i in range(1, L):
        taps = taps + recv_ref[i, T + half:, :].astype(F32)
    total = taps[0:KER]
    hi = total.astype(BF).astype(F32)
    low = total - hi
    chunk_ref[CHUNK:, :] = jnp.zeros((CROWS - CHUNK, 128), F32)
    for j in range(PEERS):
        chunk_ref[0:CHUNK, :] = flat_ref[j * CHUNK:(j + 1) * CHUNK, :]
        if j < KER * 6:
            k, b = divmod(j, 6)
            chunk_ref[CHUNK:CHUNK + 1, :] = hi[k:k + 1, b * 128:(b + 1) * 128]
            chunk_ref[CHUNK + 1:CHUNK + 2, :] = low[k:k + 1, b * 128:(b + 1) * 128]
        out_ref[j] = chunk_ref[...].astype(BF)


def sum_kernel(parts_ref, out_ref, chunk_ref):
    total = parts_ref[0].astype(F32)
    for j in range(1, PEERS):
        total = total + parts_ref[j].astype(F32)
    chunk_ref[...] = total
    tap = total[CHUNK:CHUNK + 1] + total[CHUNK + 1:CHUNK + 2]
    hi = tap.astype(BF).astype(F32)
    chunk_ref[CHUNK:CHUNK + 1, :] = hi
    chunk_ref[CHUNK + 1:CHUNK + 2, :] = tap - hi
    mine = chunk_ref[...].astype(BF)
    for j in range(PEERS):
        out_ref[j] = mine


def place_kernel(mine_ref, theirs_ref, grad_ref, taps_ref, flat_ref):
    core = lax.axis_index("c")
    for ref, which in ((mine_ref, core), (theirs_ref, 1 - core)):
        start = pl.multiple_of(which * H, H)
        for j in range(PEERS):
            flat_ref[j * CHUNK:(j + 1) * CHUNK, :] = ref[j, 0:CHUNK, :].astype(F32)
        for b in range(D // 128):
            grad_ref[0, pl.ds(start, H), b * 128:(b + 1) * 128] = (
                flat_ref[b * H:(b + 1) * H, :].astype(BF))
    for j in range(KER * 6):
        k, b = divmod(j, 6)
        pair = mine_ref[j, CHUNK:, :].astype(F32) + theirs_ref[j, CHUNK:, :].astype(F32)
        taps_ref[k, :, b * 128:(b + 1) * 128] = pair[0:1] + pair[1:2]


def params(mib):
    return pltpu.CompilerParams(vmem_limit_bytes=mib * MIB)


def body(features, lengths, front_weight, pointwise, kernel, targets):
    ring = route((2, 4), lambda c, x: (c, (x + 1 if c == 0 else x - 1) % 4))
    pair = route(
        (4, 2, 2),
        lambda h, c, z: (h, c, 1 - z) if c == 0 else ((h + 2 * z - 1) % 4, c, 1 - z),
    )

    def along_x(a):
        return lax.ppermute(a, ("c", "x"), ring)

    def along_z(a):
        return lax.ppermute(a, ("zh", "c", "zl"), pair)

    def to_core(a):
        return lax.ppermute(a, "c", [(0, 1), (1, 0)])

    near, far, io = pl.pallas_call(
        prep_kernel,
        name="prep",
        out_shape=(
            jax.ShapeDtypeStruct((NEAR, D), BF),
            jax.ShapeDtypeStruct((FAR, D), BF),
            jax.ShapeDtypeStruct((INROWS, FEAT + D), BF),
        ),
        in_specs=[ANY, VMEM, ANY, ANY, SMEM],
        out_specs=(VMEM, VMEM, VMEM),
        scratch_shapes=[pltpu.SemaphoreType.DMA((4,))],
    )(pointwise, jnp.transpose(kernel, (1, 0, 2)), features, targets, lengths)
    begin = pl.pallas_call(
        front_kernel,
        name="front",
        out_shape=jax.ShapeDtypeStruct((2 * T + INROWS - T, D), BF),
        in_specs=[VMEM, VMEM, VMEM],
        out_specs=VMEM,
    )(io, to_core(io), front_weight)

    n1, n3, begin = lax.optimization_barrier((along_x(near), along_z(near), begin))
    f1 = along_x(far)
    n2 = along_x(n1)
    n4 = along_z(n1[:H + TAPS])
    f4 = along_z(f1)
    m1, m3 = to_core(n1[:H]), to_core(n3[:H])
    n2, n4, m1, m3 = lax.optimization_barrier((n2, n4, m1, m3))
    n5 = along_z(n2[:H + TAPS])
    g1, m2, m4 = to_core(f1[:H + TAPS]), to_core(n2[:H + TAPS]), to_core(n4)
    g4, m5 = to_core(f4[:H + 8]), to_core(n5[:H])
    here = [near, far, n1, f1, n2, n3, n4, f4, n5]
    there = [m1, g1, m2, m3, m4, g4, m5]

    payload = pl.pallas_call(
        model_kernel,
        name="model",
        out_shape=jax.ShapeDtypeStruct((L, PAY, D), BF),
        in_specs=[VMEM] + [ANY] * 16,
        out_specs=VMEM,
        scratch_shapes=[
            pltpu.VMEM((L, D, D), BF),
            pltpu.VMEM((L, TAPS, D), BF),
            pltpu.VMEM((L, 8, D), F32),
            pltpu.VMEM((L, T, 128), F32),
            pltpu.VMEM((L, T + 16, D), F32),
            pltpu.VMEM((L, T, D), F32),
            pltpu.VMEM((L, T, D), BF),
            pltpu.VMEM((T + 16, D), F32),
            pltpu.VMEM((T, D), F32),
            pltpu.SemaphoreType.DMA((L,)),
            pltpu.SemaphoreType.DMA((L,)),
        ],
        compiler_params=params(28),
    )(begin, *here, *there)

    received = lax.all_to_all(payload, ("x", "zl"), 0, 0)

    parts = pl.pallas_call(
        grad_kernel,
        name="grad",
        out_shape=jax.ShapeDtypeStruct((PEERS, CROWS, 128), BF),
        in_specs=[VMEM],
        out_specs=VMEM,
        scratch_shapes=[
            pltpu.VMEM((L * T, H), BF),
            pltpu.VMEM((H * 6, 128), F32),
            pltpu.VMEM((8, D), F32),
            pltpu.VMEM((CROWS, 128), F32),
        ],
        compiler_params=params(24),
    )(received)

    scattered = lax.all_to_all(parts, ("y", "zh"), 0, 0)

    mine = pl.pallas_call(
        sum_kernel,
        name="total",
        out_shape=jax.ShapeDtypeStruct((PEERS, CROWS, 128), BF),
        in_specs=[VMEM],
        out_specs=VMEM,
        scratch_shapes=[pltpu.VMEM((CROWS, 128), F32)],
        compiler_params=params(16),
    )(scattered)

    half = lax.all_to_all(mine, ("y", "zh"), 0, 0)
    other_half = to_core(half)

    grads, tap_grads = pl.pallas_call(
        place_kernel,
        name="place",
        out_shape=(
            jax.ShapeDtypeStruct((1, D, D), BF),
            jax.ShapeDtypeStruct((KER, 1, D), F32),
        ),
        in_specs=[VMEM, VMEM],
        out_specs=(VMEM, VMEM),
        scratch_shapes=[pltpu.VMEM((H * 6, 128), F32)],
        compiler_params=params(16),
    )(half, other_half)
    return grads, jnp.transpose(tap_grads, (1, 0, 2))


def solution(mesh):
    fine = Mesh(mesh.devices.reshape(8, 4, 2, 4, 2), ("y", "zh", "c", "x", "zl"))
    dp = ("y", "zh", "c")
    section = ("x", "zl")
    return jax.shard_map(
        body,
        mesh=fine,
        in_specs=(
            P(dp, None, None),
            P(dp),
            P(),
            P(section, None, None),
            P(section, None, None),
            P(dp, None, None),
        ),
        out_specs=(P(section, None, None), P(section, None, None)),
        check_vma=False,
    )
```

```python
import itertools

import jax
import jax.numpy as jnp
from jax import lax
from jax.experimental import pallas as pl
from jax.experimental.pallas import tpu as pltpu
from jax.sharding import Mesh, PartitionSpec as P

EPS = 1e-06
BF = jnp.bfloat16
F32 = jnp.float32

D = 768
H = 384
KER = 5
FEAT = 512
T = 64
L = 8
TAPS = 16
NEAR = H + TAPS + 8
FAR = H + 2 * TAPS
START = 2 * T + 16
PAY = T + 8
ROWS = H * 6
PEERS = 32
CHUNK = 72
CROWS = 80
MIB = 1024 * 1024

VMEM = pl.BlockSpec(memory_space=pltpu.VMEM)
ANY = pl.BlockSpec(memory_space=pl.ANY)
SMEM = pl.BlockSpec(memory_space=pltpu.SMEM)


def route(shape, step):
    spots = list(itertools.product(*map(range, shape)))
    place = {spot: i for i, spot in enumerate(spots)}
    return [(place[spot], place[step(*spot)]) for spot in spots]


def split3(x):
    hi = x.astype(BF).astype(F32)
    rest = x - hi
    mid = rest.astype(BF).astype(F32)
    return hi, mid, rest - mid


def where_am_i():
    section = 2 * lax.axis_index("x") + lax.axis_index("zl")
    return section, lax.axis_index("c")


def prep_kernel(w_ref, taps_ref, near_ref, far_ref, sem):
    _, core = where_am_i()
    mine = pl.multiple_of(core * H, H)
    theirs = pl.multiple_of((1 - core) * H, H)
    copies = [
        pltpu.make_async_copy(w_ref.at[0, pl.ds(mine, H)], near_ref.at[pl.ds(0, H)], sem.at[0]),
        pltpu.make_async_copy(w_ref.at[0, pl.ds(theirs, H)], far_ref.at[pl.ds(0, H)], sem.at[1]),
    ]
    for copy in copies:
        copy.start()
    taps = jnp.concatenate([taps_ref[k] for k in range(KER)], axis=0)
    hi, mid, low = split3(taps)
    packed = jnp.concatenate([hi, mid, low, jnp.zeros((1, D), F32)], axis=0).astype(BF)
    near_ref[H:H + TAPS, :] = packed
    near_ref[H + TAPS:, :] = jnp.zeros((NEAR - H - TAPS, D), BF)
    far_ref[H:H + TAPS, :] = packed
    far_ref[H + TAPS:, :] = packed
    for copy in copies:
        copy.wait()


def front_kernel(feat_ref, front_ref, targ_ref, len_ref, out_ref):
    section, _ = where_am_i()
    utt = lax.rem(section, 4)
    out_ref[0:T, :] = jnp.dot(
        feat_ref[utt], front_ref[...], preferred_element_type=F32).astype(BF)
    out_ref[T:2 * T, :] = targ_ref[utt]
    count = len_ref[utt].astype(F32)
    out_ref[2 * T:, :] = jnp.full((START - 2 * T, D), count, F32).astype(BF)


def model_kernel(
    start_ref,
    n0, f0, n1, f1, n2, n3, f3, n4, f4, n5, m1, g1, m2, m4, g4, m5,
    pay_ref,
    w_ref, traw_ref, taps_ref, inv_ref, norm_ref, slope_ref, act_ref, gpad_ref, g_ref,
    wsem, tsem,
):
    section, core = where_am_i()
    col = lax.div(section, 2)
    row = lax.rem(section, 2)
    other = 1 - core
    side = lax.rem(col + 3 + 2 * core, 4)
    anti = lax.rem(col + 1 + 2 * core, 4)
    across = lax.rem(col + 2, 4)
    flip = 1 - row

    def bring(piece, c, r, part, with_taps):
        layer = 2 * c + r
        start = pl.multiple_of(part * H, H)
        pltpu.make_async_copy(
            piece.at[pl.ds(0, H)], w_ref.at[layer, pl.ds(start, H)], wsem.at[layer]).start()
        if with_taps:
            pltpu.make_async_copy(
                piece.at[pl.ds(H, TAPS)], traw_ref.at[layer], tsem.at[layer]).start()

    for near, far, c, r, part in (
        (n0, f0, col, row, core), (n1, f1, side, row, core),
        (n3, f3, col, flip, core), (n4, f4, side, flip, core),
    ):
        bring(near, c, r, part, False)
        bring(far, c, r, 1 - part, True)
    bring(m1, anti, row, other, False)
    bring(g1, anti, row, core, True)
    bring(m4, anti, flip, other, True)
    bring(g4, anti, flip, core, False)
    for near, mirror, r in ((n2, m2, row), (n5, m5, flip)):
        bring(near, across, r, core, True)
        bring(mirror, across, r, other, False)

    count = start_ref[2 * T:, :].astype(F32)[0:1, 0:1]
    target = start_ref[T:2 * T, :].astype(F32)
    frame = lax.broadcasted_iota(jnp.int32, (T, 1), 0).astype(F32)
    mask = jnp.where(frame < count, 1.0, 0.0).astype(F32)
    g_ref[...] = start_ref[0:T, :].astype(F32)

    edge = jnp.zeros((8, D), F32)
    gpad_ref[0:8, :] = edge
    gpad_ref[T + 8:, :] = edge

    def forward(l, carry):
        pltpu.make_async_copy(traw_ref.at[l], traw_ref.at[l], tsem.at[l]).wait()
        pltpu.make_async_copy(w_ref.at[l], w_ref.at[l], wsem.at[l]).wait()
        raw = traw_ref[l].astype(F32)
        taps = raw[0:KER] + raw[KER:2 * KER] + raw[2 * KER:3 * KER]
        taps_ref[l, 0:KER, :] = taps
        vals = g_ref[...]
        inv = lax.rsqrt(jnp.mean(vals * vals, axis=-1, keepdims=True) + EPS)
        norm = vals * (inv * mask)
        inv_ref[l] = jnp.broadcast_to(inv, (T, 128))
        norm_ref[l, 0:8, :] = edge
        norm_ref[l, T + 8:, :] = edge
        norm_ref[l, 8:T + 8, :] = norm
        conv = taps[0:1] * norm_ref[l, 6:T + 6, :]
        for k in range(1, KER):
            conv = conv + taps[k:k + 1] * norm_ref[l, 6 + k:T + 6 + k, :]
        sig = jax.nn.sigmoid(conv)
        act = (conv * sig).astype(BF)
        slope_ref[l] = sig * (1.0 + conv * (1.0 - sig))
        act_ref[l] = act
        out = vals + jnp.dot(act, w_ref[l], preferred_element_type=F32)
        g_ref[...] = out.astype(BF).astype(F32)
        return carry

    lax.fori_loop(0, L, forward, 0, unroll=True)

    g_ref[...] = ((g_ref[...] - target) * mask / count).astype(BF).astype(F32)

    first = section < 4

    def backward(i, carry):
        l = L - 1 - i
        g = g_ref[...]
        gb = g.astype(BF)
        pay_ref[l, 0:T, :] = jnp.where(first, act_ref[l].astype(F32), g).astype(BF)
        grad_act = lax.dot_general(
            gb, w_ref[l], (((1,), (1,)), ((), ())), preferred_element_type=F32)
        grad_conv = grad_act * slope_ref[l]
        gpad_ref[8:T + 8, :] = grad_conv
        taps = taps_ref[l, 0:KER, :]
        rows = []
        for k in range(KER):
            rows.append(jnp.sum(grad_conv * norm_ref[l, 6 + k:T + 6 + k, :], axis=0, keepdims=True))
        total = jnp.concatenate(rows, axis=0)
        hi = total.astype(BF).astype(F32)
        part = jnp.where(first, hi, total - hi)
        packed = jnp.concatenate([part, jnp.zeros((8 - KER, D), F32)], axis=0)
        pay_ref[l, T:, :] = packed.astype(BF)
        grad_norm = taps[0:1] * gpad_ref[10:T + 10, :]
        for k in range(1, KER):
            grad_norm = grad_norm + taps[k:k + 1] * gpad_ref[10 - k:T + 10 - k, :]
        grad_norm = grad_norm * mask
        inv = inv_ref[l][:, 0:1]
        norm = norm_ref[l, 8:T + 8, :]
        mean = jnp.mean(grad_norm * norm, axis=-1, keepdims=True)
        g_ref[...] = (g + inv * (grad_norm - norm * mean)).astype(BF).astype(F32)
        return carry

    lax.fori_loop(0, L, backward, 0, unroll=True)


def half_product(recv_ref, part, out_ref):
    start = pl.multiple_of(part * H, H)
    act = recv_ref[0:4, 0:T, pl.ds(start, H)].reshape(4 * T, H)
    cot = recv_ref[4:8, 0:T, :].reshape(4 * T, D)
    grad = lax.dot_general(act, cot, (((0,), (0,)), ((), ())), preferred_element_type=F32)
    for b in range(D // 128):
        out_ref[b * H:(b + 1) * H, :] = grad[:, b * 128:(b + 1) * 128].astype(out_ref.dtype)


def lend_kernel(recv_ref, out_ref):
    half_product(recv_ref, 1 - lax.axis_index("c"), out_ref)


def grad_kernel(recv_ref, lent_ref, out_ref, flat_ref, chunk_ref):
    half_product(recv_ref, lax.axis_index("c"), flat_ref)
    taps = recv_ref[0, T:, :].astype(F32)
    for i in range(1, L):
        taps = taps + recv_ref[i, T:, :].astype(F32)
    total = taps[0:KER]
    hi = total.astype(BF).astype(F32)
    low = total - hi
    chunk_ref[CHUNK:, :] = jnp.zeros((CROWS - CHUNK, 128), F32)
    flat_ref[...] = flat_ref[...] + lent_ref[...].astype(F32)
    for j in range(PEERS):
        chunk_ref[0:CHUNK, :] = flat_ref[j * CHUNK:(j + 1) * CHUNK, :]
        if j < KER * 6:
            k, b = divmod(j, 6)
            chunk_ref[CHUNK:CHUNK + 1, :] = hi[k:k + 1, b * 128:(b + 1) * 128]
            chunk_ref[CHUNK + 1:CHUNK + 2, :] = low[k:k + 1, b * 128:(b + 1) * 128]
        out_ref[j] = chunk_ref[...].astype(BF)


def sum_kernel(parts_ref, out_ref, chunk_ref):
    total = parts_ref[0].astype(F32)
    for j in range(1, PEERS):
        total = total + parts_ref[j].astype(F32)
    chunk_ref[...] = total
    tap = total[CHUNK:CHUNK + 1] + total[CHUNK + 1:CHUNK + 2]
    hi = tap.astype(BF).astype(F32)
    chunk_ref[CHUNK:CHUNK + 1, :] = hi
    chunk_ref[CHUNK + 1:CHUNK + 2, :] = tap - hi
    mine = chunk_ref[...].astype(BF)
    for j in range(PEERS):
        out_ref[j] = mine


def place_kernel(mine_ref, theirs_ref, grad_ref, taps_ref, flat_ref):
    core = lax.axis_index("c")
    for ref, which in ((mine_ref, core), (theirs_ref, 1 - core)):
        start = pl.multiple_of(which * H, H)
        for j in range(PEERS):
            flat_ref[j * CHUNK:(j + 1) * CHUNK, :] = ref[j, 0:CHUNK, :].astype(F32)
        for b in range(D // 128):
            grad_ref[0, pl.ds(start, H), b * 128:(b + 1) * 128] = (
                flat_ref[b * H:(b + 1) * H, :].astype(BF))
    for j in range(KER * 6):
        k, b = divmod(j, 6)
        pair = mine_ref[j, CHUNK:, :].astype(F32) + theirs_ref[j, CHUNK:, :].astype(F32)
        taps_ref[k, :, b * 128:(b + 1) * 128] = pair[0:1] + pair[1:2]


def params(mib):
    return pltpu.CompilerParams(vmem_limit_bytes=mib * MIB)


def body(features, lengths, front_weight, pointwise, kernel, targets):
    ring = route((2, 4), lambda c, x: (c, (x + 1 if c == 0 else x - 1) % 4))
    pair = route(
        (4, 2, 2),
        lambda h, c, z: (h, c, 1 - z) if c == 0 else ((h + 2 * z - 1) % 4, c, 1 - z),
    )

    def along_x(a):
        return lax.ppermute(a, ("c", "x"), ring)

    def along_z(a):
        return lax.ppermute(a, ("zh", "c", "zl"), pair)

    def to_core(a):
        return lax.ppermute(a, "c", [(0, 1), (1, 0)])

    near, far = pl.pallas_call(
        prep_kernel,
        name="prep",
        out_shape=(jax.ShapeDtypeStruct((NEAR, D), BF), jax.ShapeDtypeStruct((FAR, D), BF)),
        in_specs=[ANY, VMEM],
        out_specs=(VMEM, VMEM),
        scratch_shapes=[pltpu.SemaphoreType.DMA((2,))],
    )(pointwise, jnp.transpose(kernel, (1, 0, 2)))
    begin = pl.pallas_call(
        front_kernel,
        name="front",
        out_shape=jax.ShapeDtypeStruct((START, D), BF),
        in_specs=[VMEM, VMEM, VMEM, SMEM],
        out_specs=VMEM,
    )(features, front_weight, targets, lengths)

    n1, n3, begin = lax.optimization_barrier((along_x(near), along_z(near), begin))
    f1, f3 = along_x(far), along_z(far)
    n2 = along_x(n1)
    n4 = along_z(n1[:H + TAPS])
    f4 = along_x(f3)
    m1 = to_core(n1[:H])
    n2, n4, m1, f1 = lax.optimization_barrier((n2, n4, m1, f1))
    n5 = along_z(n2[:H + TAPS])
    g1, m2, m4 = to_core(f1[:H + TAPS]), to_core(n2[:H + TAPS]), to_core(n4)
    g4, m5 = to_core(f4[:H + 8]), to_core(n5[:H])
    here = [near, far, n1, f1, n2, n3, f3, n4, f4, n5]
    there = [m1, g1, m2, m4, g4, m5]

    payload = pl.pallas_call(
        model_kernel,
        name="model",
        out_shape=jax.ShapeDtypeStruct((L, PAY, D), BF),
        in_specs=[VMEM] + [ANY] * 16,
        out_specs=VMEM,
        scratch_shapes=[
            pltpu.VMEM((L, D, D), BF),
            pltpu.VMEM((L, TAPS, D), BF),
            pltpu.VMEM((L, 8, D), F32),
            pltpu.VMEM((L, T, 128), F32),
            pltpu.VMEM((L, T + 16, D), F32),
            pltpu.VMEM((L, T, D), F32),
            pltpu.VMEM((L, T, D), BF),
            pltpu.VMEM((T + 16, D), F32),
            pltpu.VMEM((T, D), F32),
            pltpu.SemaphoreType.DMA((L,)),
            pltpu.SemaphoreType.DMA((L,)),
        ],
        compiler_params=params(28),
    )(begin, *here, *there)

    received = lax.all_to_all(payload, ("x", "zl"), 0, 0)

    lend = pl.pallas_call(
        lend_kernel,
        name="lend",
        out_shape=jax.ShapeDtypeStruct((ROWS, 128), BF),
        in_specs=[VMEM],
        out_specs=VMEM,
        compiler_params=params(24),
    )(received)
    parts = pl.pallas_call(
        grad_kernel,
        name="grad",
        out_shape=jax.ShapeDtypeStruct((PEERS, CROWS, 128), BF),
        in_specs=[VMEM, VMEM],
        out_specs=VMEM,
        scratch_shapes=[pltpu.VMEM((ROWS, 128), F32), pltpu.VMEM((CROWS, 128), F32)],
        compiler_params=params(24),
    )(received, to_core(lend))

    scattered = lax.all_to_all(parts, ("y", "zh"), 0, 0)

    mine = pl.pallas_call(
        sum_kernel,
        name="total",
        out_shape=jax.ShapeDtypeStruct((PEERS, CROWS, 128), BF),
        in_specs=[VMEM],
        out_specs=VMEM,
        scratch_shapes=[pltpu.VMEM((CROWS, 128), F32)],
        compiler_params=params(16),
    )(scattered)

    half = lax.all_to_all(mine, ("y", "zh"), 0, 0)
    other_half = to_core(half)

    grads, tap_grads = pl.pallas_call(
        place_kernel,
        name="place",
        out_shape=(
            jax.ShapeDtypeStruct((1, D, D), BF),
            jax.ShapeDtypeStruct((KER, 1, D), F32),
        ),
        in_specs=[VMEM, VMEM],
        out_specs=(VMEM, VMEM),
        scratch_shapes=[pltpu.VMEM((H * 6, 128), F32)],
        compiler_params=params(16),
    )(half, other_half)
    return grads, jnp.transpose(tap_grads, (1, 0, 2))


def solution(mesh):
    fine = Mesh(mesh.devices.reshape(8, 4, 2, 4, 2), ("y", "zh", "c", "x", "zl"))
    dp = ("y", "zh", "c")
    section = ("x", "zl")
    return jax.shard_map(
        body,
        mesh=fine,
        in_specs=(
            P(dp, None, None),
            P(dp),
            P(),
            P(section, None, None),
            P(section, None, None),
            P(dp, None, None),
        ),
        out_specs=(P(section, None, None), P(section, None, None)),
        check_vma=False,
    )
```

```python
import functools
import itertools

import jax
import jax.numpy as jnp
from jax import lax
from jax.experimental import pallas as pl
from jax.experimental.pallas import tpu as pltpu
from jax.sharding import Mesh, PartitionSpec as P

EPS = 1e-06
BF = jnp.bfloat16
F32 = jnp.float32

D = 768
H = 384
KER = 5
FEAT = 512
T = 64
L = 8
TAPS = 16
NEAR = H + TAPS + 8
FAR = H + 2 * TAPS
START = 2 * T + 16
PAY = T + 8
ROWS = H * 6
PEERS = 32
CHUNK = 72
CROWS = 80
MIB = 1024 * 1024
BLOCKS = [slice(i, i + H) for i in range(0, D, H)]

VMEM = pl.BlockSpec(memory_space=pltpu.VMEM)
ANY = pl.BlockSpec(memory_space=pl.ANY)
SMEM = pl.BlockSpec(memory_space=pltpu.SMEM)


def route(shape, step):
    spots = list(itertools.product(*map(range, shape)))
    place = {spot: i for i, spot in enumerate(spots)}
    return [(place[spot], place[step(*spot)]) for spot in spots]


def split3(x):
    hi = x.astype(BF).astype(F32)
    rest = x - hi
    mid = rest.astype(BF).astype(F32)
    return hi, mid, rest - mid


def where_am_i():
    section = 2 * lax.axis_index("x") + lax.axis_index("zl")
    return section, lax.axis_index("c")


def prep_kernel(far, w_ref, taps_ref, out_ref, sem):
    core = lax.axis_index("c")
    part = pl.multiple_of((1 - core if far else core) * H, H)
    copy = pltpu.make_async_copy(w_ref.at[0, pl.ds(part, H)], out_ref.at[pl.ds(0, H)], sem)
    copy.start()
    taps = jnp.concatenate([taps_ref[k] for k in range(KER)], axis=0)
    hi, mid, low = split3(taps)
    packed = jnp.concatenate([hi, mid, low, jnp.zeros((1, D), F32)], axis=0).astype(BF)
    out_ref[H:H + TAPS, :] = packed
    out_ref[H + TAPS:, :] = jnp.zeros((out_ref.shape[0] - H - TAPS, D), BF)
    copy.wait()


def front_kernel(feat_ref, front_ref, targ_ref, len_ref, out_ref):
    section, _ = where_am_i()
    utt = lax.rem(section, 4)
    out_ref[0:T, :] = jnp.dot(
        feat_ref[utt], front_ref[...], preferred_element_type=F32).astype(BF)
    out_ref[T:2 * T, :] = targ_ref[utt]
    count = len_ref[utt].astype(F32)
    out_ref[2 * T:, :] = jnp.full((START - 2 * T, D), count, F32).astype(BF)


def model_kernel(
    start_ref,
    n0, f0, n1, f1, n2, n3, f3, n4, f4, n5, m1, m2, g4, m5,
    pay_ref,
    w_ref, traw_ref, taps_ref, inv_ref, norm_ref, slope_ref, act_ref, gpad_ref, g_ref,
    wsem, tsem,
):
    section, core = where_am_i()
    col = lax.div(section, 2)
    row = lax.rem(section, 2)
    other = 1 - core
    side = lax.rem(col + 3 + 2 * core, 4)
    anti = lax.rem(col + 1 + 2 * core, 4)
    across = lax.rem(col + 2, 4)
    flip = 1 - row

    def bring(piece, first, c, r, part, taps_at):
        layer = 2 * c + r
        start = pl.multiple_of(part * H, H)
        pltpu.make_async_copy(
            piece.at[pl.ds(first, H)], w_ref.at[layer, pl.ds(start, H)], wsem.at[layer]).start()
        if taps_at is not None:
            pltpu.make_async_copy(
                piece.at[pl.ds(taps_at, TAPS)], traw_ref.at[layer], tsem.at[layer]).start()

    for near, far, c, r in (
        (n0, f0, col, row), (n1, f1, side, row), (n3, f3, col, flip), (n4, f4, side, flip),
    ):
        bring(near, 0, c, r, core, H)
        bring(far, 0, c, r, other, None)
    bring(m1, 0, anti, row, other, H)
    bring(m1, H + TAPS, anti, row, core, None)
    bring(m2, H, anti, flip, other, 2 * H)
    bring(g4, 0, anti, flip, core, None)
    bring(n2, 0, across, row, core, H)
    bring(m2, 0, across, row, other, None)
    bring(n5, 0, across, flip, core, H)
    bring(m5, 0, across, flip, other, None)

    count = start_ref[2 * T:, :].astype(F32)[0:1, 0:1]
    target = start_ref[T:2 * T, :].astype(F32)
    frame = lax.broadcasted_iota(jnp.int32, (T, 1), 0).astype(F32)
    mask = jnp.where(frame < count, 1.0, 0.0).astype(F32)
    g_ref[...] = start_ref[0:T, :].astype(F32)

    edge = jnp.zeros((8, D), F32)
    gpad_ref[0:8, :] = edge
    gpad_ref[T + 8:, :] = edge

    def forward(l, carry):
        pltpu.make_async_copy(traw_ref.at[l], traw_ref.at[l], tsem.at[l]).wait()
        pltpu.make_async_copy(w_ref.at[l], w_ref.at[l], wsem.at[l]).wait()
        raw = traw_ref[l].astype(F32)
        taps = raw[0:KER] + raw[KER:2 * KER] + raw[2 * KER:3 * KER]
        taps_ref[l, 0:KER, :] = taps
        vals = g_ref[...]
        inv = lax.rsqrt(jnp.mean(vals * vals, axis=-1, keepdims=True) + EPS)
        inv_ref[l] = jnp.broadcast_to(inv, (T, 128))
        scale = inv * mask
        norm_ref[l, 0:8, :] = edge
        norm_ref[l, T + 8:, :] = edge
        out = vals
        for block in BLOCKS:
            norm_ref[l, 8:T + 8, block] = vals[:, block] * scale
            conv = taps[0:1, block] * norm_ref[l, 6:T + 6, block]
            for k in range(1, KER):
                conv = conv + taps[k:k + 1, block] * norm_ref[l, 6 + k:T + 6 + k, block]
            sig = jax.nn.sigmoid(conv)
            act = (conv * sig).astype(BF)
            slope_ref[l, :, block] = sig * (1.0 + conv * (1.0 - sig))
            act_ref[l, :, block] = act
            out = out + jnp.dot(act, w_ref[l, block, :], preferred_element_type=F32)
        g_ref[...] = out.astype(BF).astype(F32)
        return carry

    lax.fori_loop(0, L, forward, 0, unroll=True)

    g_ref[...] = ((g_ref[...] - target) * mask / count).astype(BF).astype(F32)

    first = section < 4

    def backward(i, carry):
        l = L - 1 - i
        g = g_ref[...]
        gb = g.astype(BF)
        pay_ref[l, 0:T, :] = jnp.where(first, act_ref[l].astype(F32), g).astype(BF)
        inv = inv_ref[l][:, 0:1]
        taps = taps_ref[l, 0:KER, :]
        grads, mean = [], 0.0
        for block in BLOCKS:
            grad_act = lax.dot_general(
                gb, w_ref[l, block, :], (((1,), (1,)), ((), ())), preferred_element_type=F32)
            grad_conv = grad_act * slope_ref[l, :, block]
            gpad_ref[8:T + 8, block] = grad_conv
            rows = []
            for k in range(KER):
                rows.append(jnp.sum(
                    grad_conv * norm_ref[l, 6 + k:T + 6 + k, block], axis=0, keepdims=True))
            total = jnp.concatenate(rows, axis=0)
            hi = total.astype(BF).astype(F32)
            part = jnp.where(first, hi, total - hi)
            part = jnp.concatenate([part, jnp.zeros((8 - KER, part.shape[1]), F32)], axis=0)
            pay_ref[l, T:, block] = part.astype(BF)
            grad_norm = taps[0:1, block] * gpad_ref[10:T + 10, block]
            for k in range(1, KER):
                grad_norm = grad_norm + taps[k:k + 1, block] * gpad_ref[10 - k:T + 10 - k, block]
            grad_norm = grad_norm * mask
            grads.append(grad_norm)
            mean = mean + jnp.sum(
                grad_norm * norm_ref[l, 8:T + 8, block], axis=-1, keepdims=True)
        mean = mean * (1.0 / D)
        for block, grad_norm in zip(BLOCKS, grads):
            norm = norm_ref[l, 8:T + 8, block]
            g_ref[:, block] = (
                g[:, block] + inv * (grad_norm - norm * mean)).astype(BF).astype(F32)
        return carry

    lax.fori_loop(0, L, backward, 0, unroll=True)


def half_product(recv_ref, part, out_ref):
    start = pl.multiple_of(part * H, H)
    act = recv_ref[0:4, 0:T, pl.ds(start, H)].reshape(4 * T, H)
    cot = recv_ref[4:8, 0:T, :].reshape(4 * T, D)
    grad = lax.dot_general(act, cot, (((0,), (0,)), ((), ())), preferred_element_type=F32)
    for b in range(D // 128):
        out_ref[b * H:(b + 1) * H, :] = grad[:, b * 128:(b + 1) * 128].astype(out_ref.dtype)


def lend_kernel(recv_ref, out_ref):
    half_product(recv_ref, 1 - lax.axis_index("c"), out_ref)


def grad_kernel(recv_ref, lent_ref, out_ref, flat_ref, chunk_ref):
    half_product(recv_ref, lax.axis_index("c"), flat_ref)
    taps = recv_ref[0, T:, :].astype(F32)
    for i in range(1, L):
        taps = taps + recv_ref[i, T:, :].astype(F32)
    total = taps[0:KER]
    hi = total.astype(BF).astype(F32)
    low = total - hi
    chunk_ref[CHUNK:, :] = jnp.zeros((CROWS - CHUNK, 128), F32)
    flat_ref[...] = flat_ref[...] + lent_ref[...].astype(F32)
    for j in range(PEERS):
        chunk_ref[0:CHUNK, :] = flat_ref[j * CHUNK:(j + 1) * CHUNK, :]
        if j < KER * 6:
            k, b = divmod(j, 6)
            chunk_ref[CHUNK:CHUNK + 1, :] = hi[k:k + 1, b * 128:(b + 1) * 128]
            chunk_ref[CHUNK + 1:CHUNK + 2, :] = low[k:k + 1, b * 128:(b + 1) * 128]
        out_ref[j] = chunk_ref[...].astype(BF)


def sum_kernel(parts_ref, out_ref, chunk_ref):
    total = parts_ref[0].astype(F32)
    for j in range(1, PEERS):
        total = total + parts_ref[j].astype(F32)
    chunk_ref[...] = total
    tap = total[CHUNK:CHUNK + 1] + total[CHUNK + 1:CHUNK + 2]
    hi = tap.astype(BF).astype(F32)
    chunk_ref[CHUNK:CHUNK + 1, :] = hi
    chunk_ref[CHUNK + 1:CHUNK + 2, :] = tap - hi
    mine = chunk_ref[...].astype(BF)
    for j in range(PEERS):
        out_ref[j] = mine


def place_kernel(mine_ref, theirs_ref, grad_ref, taps_ref, flat_ref):
    core = lax.axis_index("c")
    for ref, which in ((mine_ref, core), (theirs_ref, 1 - core)):
        start = pl.multiple_of(which * H, H)
        for j in range(PEERS):
            flat_ref[j * CHUNK:(j + 1) * CHUNK, :] = ref[j, 0:CHUNK, :].astype(F32)
        for b in range(D // 128):
            grad_ref[0, pl.ds(start, H), b * 128:(b + 1) * 128] = (
                flat_ref[b * H:(b + 1) * H, :].astype(BF))
    for j in range(KER * 6):
        k, b = divmod(j, 6)
        pair = mine_ref[j, CHUNK:, :].astype(F32) + theirs_ref[j, CHUNK:, :].astype(F32)
        taps_ref[k, :, b * 128:(b + 1) * 128] = pair[0:1] + pair[1:2]


def params(mib):
    return pltpu.CompilerParams(vmem_limit_bytes=mib * MIB)


def body(features, lengths, front_weight, pointwise, kernel, targets):
    ring = route((2, 4), lambda c, x: (c, (x + 1 if c == 0 else x - 1) % 4))
    pair = route(
        (4, 2, 2),
        lambda h, c, z: (h, c, 1 - z) if c == 0 else ((h + 2 * z - 1) % 4, c, 1 - z),
    )

    def along_x(a):
        return lax.ppermute(a, ("c", "x"), ring)

    def along_z(a):
        return lax.ppermute(a, ("zh", "c", "zl"), pair)

    def to_core(a):
        return lax.ppermute(a, "c", [(0, 1), (1, 0)])

    flat_taps = jnp.transpose(kernel, (1, 0, 2))

    def prepare(far, rows):
        return pl.pallas_call(
            functools.partial(prep_kernel, far),
            name="far" if far else "near",
            out_shape=jax.ShapeDtypeStruct((rows, D), BF),
            in_specs=[ANY, VMEM],
            out_specs=VMEM,
            scratch_shapes=[pltpu.SemaphoreType.DMA],
        )(pointwise, flat_taps)

    near, far = prepare(False, NEAR), prepare(True, FAR)
    begin = pl.pallas_call(
        front_kernel,
        name="front",
        out_shape=jax.ShapeDtypeStruct((START, D), BF),
        in_specs=[VMEM, VMEM, VMEM, SMEM],
        out_specs=VMEM,
    )(features, front_weight, targets, lengths)

    n1, n3, begin = lax.optimization_barrier((along_x(near), along_z(near), begin))
    f1, f3 = along_x(far), along_z(far)
    n2 = along_x(n1)
    n4 = along_z(n1[:H + TAPS])
    f4 = along_x(f3)
    n2, n4, f1 = lax.optimization_barrier((n2, n4, f1))
    n5 = along_z(n2)
    m1 = to_core(jnp.concatenate([n1[:H + TAPS], f1[:H]], axis=0))
    m2 = to_core(jnp.concatenate([n2[:H], n4], axis=0))
    g4, m5 = to_core(f4[:H + 8]), to_core(n5[:H])
    here = [near, far, n1, f1, n2, n3, f3, n4, f4, n5]
    there = [m1, m2, g4, m5]

    payload = pl.pallas_call(
        model_kernel,
        name="model",
        out_shape=jax.ShapeDtypeStruct((L, PAY, D), BF),
        in_specs=[VMEM] + [ANY] * 14,
        out_specs=VMEM,
        scratch_shapes=[
            pltpu.VMEM((L, D, D), BF),
            pltpu.VMEM((L, TAPS, D), BF),
            pltpu.VMEM((L, 8, D), F32),
            pltpu.VMEM((L, T, 128), F32),
            pltpu.VMEM((L, T + 16, D), F32),
            pltpu.VMEM((L, T, D), F32),
            pltpu.VMEM((L, T, D), BF),
            pltpu.VMEM((T + 16, D), F32),
            pltpu.VMEM((T, D), F32),
            pltpu.SemaphoreType.DMA((L,)),
            pltpu.SemaphoreType.DMA((L,)),
        ],
        compiler_params=params(28),
    )(begin, *here, *there)

    received = lax.all_to_all(payload, ("x", "zl"), 0, 0)

    lend = pl.pallas_call(
        lend_kernel,
        name="lend",
        out_shape=jax.ShapeDtypeStruct((ROWS, 128), BF),
        in_specs=[VMEM],
        out_specs=VMEM,
        compiler_params=params(24),
    )(received)
    parts = pl.pallas_call(
        grad_kernel,
        name="grad",
        out_shape=jax.ShapeDtypeStruct((PEERS, CROWS, 128), BF),
        in_specs=[VMEM, VMEM],
        out_specs=VMEM,
        scratch_shapes=[pltpu.VMEM((ROWS, 128), F32), pltpu.VMEM((CROWS, 128), F32)],
        compiler_params=params(24),
    )(received, to_core(lend))

    scattered = lax.all_to_all(parts, ("y", "zh"), 0, 0)

    mine = pl.pallas_call(
        sum_kernel,
        name="total",
        out_shape=jax.ShapeDtypeStruct((PEERS, CROWS, 128), BF),
        in_specs=[VMEM],
        out_specs=VMEM,
        scratch_shapes=[pltpu.VMEM((CROWS, 128), F32)],
        compiler_params=params(16),
    )(scattered)

    half = lax.all_to_all(mine, ("y", "zh"), 0, 0)
    other_half = to_core(half)

    grads, tap_grads = pl.pallas_call(
        place_kernel,
        name="place",
        out_shape=(
            jax.ShapeDtypeStruct((1, D, D), BF),
            jax.ShapeDtypeStruct((KER, 1, D), F32),
        ),
        in_specs=[VMEM, VMEM],
        out_specs=(VMEM, VMEM),
        scratch_shapes=[pltpu.VMEM((H * 6, 128), F32)],
        compiler_params=params(16),
    )(half, other_half)
    return grads, jnp.transpose(tap_grads, (1, 0, 2))


def solution(mesh):
    fine = Mesh(mesh.devices.reshape(8, 4, 2, 4, 2), ("y", "zh", "c", "x", "zl"))
    dp = ("y", "zh", "c")
    section = ("x", "zl")
    return jax.shard_map(
        body,
        mesh=fine,
        in_specs=(
            P(dp, None, None),
            P(dp),
            P(),
            P(section, None, None),
            P(section, None, None),
            P(dp, None, None),
        ),
        out_specs=(P(section, None, None), P(section, None, None)),
        check_vma=False,
    )
```

```python
import functools
import itertools

import jax
import jax.numpy as jnp
from jax import lax
from jax.experimental import pallas as pl
from jax.experimental.pallas import tpu as pltpu
from jax.sharding import PartitionSpec as P

EPS = 1e-06
BF = jnp.bfloat16
F32 = jnp.float32

D = 768
H = 384
KER = 5
FEAT = 512
T = 64
L = 8
TAPS = 16
NEAR = H + TAPS + 8
FAR = H + 2 * TAPS
START = 2 * T + 16
PAY = T + 8
ROWS = H * 6
PEERS = 32
CHUNK = 72
CROWS = 80
MIB = 1024 * 1024
BLOCKS = [slice(i, i + H) for i in range(0, D, H)]

VMEM = pl.BlockSpec(memory_space=pltpu.VMEM)
ANY = pl.BlockSpec(memory_space=pl.ANY)
SMEM = pl.BlockSpec(memory_space=pltpu.SMEM)


def route(shape, step):
    spots = list(itertools.product(*map(range, shape)))
    place = {spot: i for i, spot in enumerate(spots)}
    return [(place[spot], place[step(*spot)]) for spot in spots]


def split3(x):
    hi = x.astype(BF).astype(F32)
    rest = x - hi
    mid = rest.astype(BF).astype(F32)
    return hi, mid, rest - mid


def which_core():
    return lax.rem(lax.axis_index("dp"), 2)


def where_am_i():
    return lax.axis_index("section"), which_core()


def prep_kernel(far, w_ref, taps_ref, out_ref, sem):
    core = which_core()
    part = pl.multiple_of((1 - core if far else core) * H, H)
    copy = pltpu.make_async_copy(w_ref.at[0, pl.ds(part, H)], out_ref.at[pl.ds(0, H)], sem)
    copy.start()
    taps = jnp.concatenate([taps_ref[k] for k in range(KER)], axis=0)
    hi, mid, low = split3(taps)
    packed = jnp.concatenate([hi, mid, low, jnp.zeros((1, D), F32)], axis=0).astype(BF)
    out_ref[H:H + TAPS, :] = packed
    out_ref[H + TAPS:, :] = jnp.zeros((out_ref.shape[0] - H - TAPS, D), BF)
    copy.wait()


def front_kernel(feat_ref, front_ref, targ_ref, len_ref, out_ref):
    section, _ = where_am_i()
    utt = lax.rem(section, 4)
    out_ref[0:T, :] = jnp.dot(
        feat_ref[utt], front_ref[...], preferred_element_type=F32).astype(BF)
    out_ref[T:2 * T, :] = targ_ref[utt]
    count = len_ref[utt].astype(F32)
    out_ref[2 * T:, :] = jnp.full((START - 2 * T, D), count, F32).astype(BF)


def model_kernel(
    start_ref,
    n0, f0, n1, f1, n2, n3, f3, n4, f4, n5, m1, m2, g4, m5,
    pay_ref,
    w_ref, traw_ref, taps_ref, inv_ref, norm_ref, slope_ref, act_ref, gpad_ref, g_ref,
    wsem, tsem,
):
    section, core = where_am_i()
    col = lax.div(section, 2)
    row = lax.rem(section, 2)
    other = 1 - core
    side = lax.rem(col + 3 + 2 * core, 4)
    anti = lax.rem(col + 1 + 2 * core, 4)
    across = lax.rem(col + 2, 4)
    flip = 1 - row

    def bring(piece, first, c, r, part, taps_at):
        layer = 2 * c + r
        start = pl.multiple_of(part * H, H)
        pltpu.make_async_copy(
            piece.at[pl.ds(first, H)], w_ref.at[layer, pl.ds(start, H)], wsem.at[layer]).start()
        if taps_at is not None:
            pltpu.make_async_copy(
                piece.at[pl.ds(taps_at, TAPS)], traw_ref.at[layer], tsem.at[layer]).start()

    for near, far, c, r in (
        (n0, f0, col, row), (n1, f1, side, row), (n3, f3, col, flip), (n4, f4, side, flip),
    ):
        bring(near, 0, c, r, core, H)
        bring(far, 0, c, r, other, None)
    bring(m1, 0, anti, row, other, H)
    bring(m1, H + TAPS, anti, row, core, None)
    bring(m2, H, anti, flip, other, 2 * H)
    bring(g4, 0, anti, flip, core, None)
    bring(n2, 0, across, row, core, H)
    bring(m2, 0, across, row, other, None)
    bring(n5, 0, across, flip, core, H)
    bring(m5, 0, across, flip, other, None)

    count = start_ref[2 * T:, :].astype(F32)[0:1, 0:1]
    target = start_ref[T:2 * T, :].astype(F32)
    frame = lax.broadcasted_iota(jnp.int32, (T, 1), 0).astype(F32)
    mask = jnp.where(frame < count, 1.0, 0.0).astype(F32)
    g_ref[...] = start_ref[0:T, :].astype(F32)

    edge = jnp.zeros((8, D), F32)
    gpad_ref[0:8, :] = edge
    gpad_ref[T + 8:, :] = edge

    def forward(l, carry):
        pltpu.make_async_copy(traw_ref.at[l], traw_ref.at[l], tsem.at[l]).wait()
        pltpu.make_async_copy(w_ref.at[l], w_ref.at[l], wsem.at[l]).wait()
        raw = traw_ref[l].astype(F32)
        taps = raw[0:KER] + raw[KER:2 * KER] + raw[2 * KER:3 * KER]
        taps_ref[l, 0:KER, :] = taps
        vals = g_ref[...]
        inv = lax.rsqrt(jnp.mean(vals * vals, axis=-1, keepdims=True) + EPS)
        inv_ref[l] = jnp.broadcast_to(inv, (T, 128))
        scale = inv * mask
        norm_ref[l, 0:8, :] = edge
        norm_ref[l, T + 8:, :] = edge
        out = vals
        for block in BLOCKS:
            norm_ref[l, 8:T + 8, block] = vals[:, block] * scale
            conv = taps[0:1, block] * norm_ref[l, 6:T + 6, block]
            for k in range(1, KER):
                conv = conv + taps[k:k + 1, block] * norm_ref[l, 6 + k:T + 6 + k, block]
            sig = jax.nn.sigmoid(conv)
            act = (conv * sig).astype(BF)
            slope_ref[l, :, block] = sig * (1.0 + conv * (1.0 - sig))
            act_ref[l, :, block] = act
            out = out + jnp.dot(act, w_ref[l, block, :], preferred_element_type=F32)
        g_ref[...] = out.astype(BF).astype(F32)
        return carry

    lax.fori_loop(0, L, forward, 0, unroll=True)

    g_ref[...] = ((g_ref[...] - target) * mask / count).astype(BF).astype(F32)

    first = section < 4

    def backward(i, carry):
        l = L - 1 - i
        g = g_ref[...]
        gb = g.astype(BF)
        pay_ref[l, 0:T, :] = jnp.where(first, act_ref[l].astype(F32), g).astype(BF)
        inv = inv_ref[l][:, 0:1]
        taps = taps_ref[l, 0:KER, :]
        grads, mean = [], 0.0
        for block in BLOCKS:
            grad_act = lax.dot_general(
                gb, w_ref[l, block, :], (((1,), (1,)), ((), ())), preferred_element_type=F32)
            grad_conv = grad_act * slope_ref[l, :, block]
            gpad_ref[8:T + 8, block] = grad_conv
            rows = []
            for k in range(KER):
                rows.append(jnp.sum(
                    grad_conv * norm_ref[l, 6 + k:T + 6 + k, block], axis=0, keepdims=True))
            total = jnp.concatenate(rows, axis=0)
            hi = total.astype(BF).astype(F32)
            part = jnp.where(first, hi, total - hi)
            part = jnp.concatenate([part, jnp.zeros((8 - KER, part.shape[1]), F32)], axis=0)
            pay_ref[l, T:, block] = part.astype(BF)
            grad_norm = taps[0:1, block] * gpad_ref[10:T + 10, block]
            for k in range(1, KER):
                grad_norm = grad_norm + taps[k:k + 1, block] * gpad_ref[10 - k:T + 10 - k, block]
            grad_norm = grad_norm * mask
            grads.append(grad_norm)
            mean = mean + jnp.sum(
                grad_norm * norm_ref[l, 8:T + 8, block], axis=-1, keepdims=True)
        mean = mean * (1.0 / D)
        for block, grad_norm in zip(BLOCKS, grads):
            norm = norm_ref[l, 8:T + 8, block]
            g_ref[:, block] = (
                g[:, block] + inv * (grad_norm - norm * mean)).astype(BF).astype(F32)
        return carry

    lax.fori_loop(0, L, backward, 0, unroll=True)


def half_product(recv_ref, part, out_ref):
    start = pl.multiple_of(part * H, H)
    act = recv_ref[0:4, 0:T, pl.ds(start, H)].reshape(4 * T, H)
    cot = recv_ref[4:8, 0:T, :].reshape(4 * T, D)
    grad = lax.dot_general(act, cot, (((0,), (0,)), ((), ())), preferred_element_type=F32)
    for b in range(D // 128):
        out_ref[b * H:(b + 1) * H, :] = grad[:, b * 128:(b + 1) * 128].astype(out_ref.dtype)


def lend_kernel(recv_ref, out_ref):
    half_product(recv_ref, 1 - which_core(), out_ref)


def grad_kernel(recv_ref, lent_ref, out_ref, flat_ref, chunk_ref):
    half_product(recv_ref, which_core(), flat_ref)
    taps = recv_ref[0, T:, :].astype(F32)
    for i in range(1, L):
        taps = taps + recv_ref[i, T:, :].astype(F32)
    total = taps[0:KER]
    hi = total.astype(BF).astype(F32)
    low = total - hi
    chunk_ref[CHUNK:, :] = jnp.zeros((CROWS - CHUNK, 128), F32)
    flat_ref[...] = flat_ref[...] + lent_ref[...].astype(F32)
    for j in range(PEERS):
        chunk_ref[0:CHUNK, :] = flat_ref[j * CHUNK:(j + 1) * CHUNK, :]
        if j < KER * 6:
            k, b = divmod(j, 6)
            chunk_ref[CHUNK:CHUNK + 1, :] = hi[k:k + 1, b * 128:(b + 1) * 128]
            chunk_ref[CHUNK + 1:CHUNK + 2, :] = low[k:k + 1, b * 128:(b + 1) * 128]
        out_ref[j] = chunk_ref[...].astype(BF)


def sum_kernel(parts_ref, out_ref, chunk_ref):
    total = parts_ref[0].astype(F32)
    for j in range(1, PEERS):
        total = total + parts_ref[j].astype(F32)
    chunk_ref[...] = total
    tap = total[CHUNK:CHUNK + 1] + total[CHUNK + 1:CHUNK + 2]
    hi = tap.astype(BF).astype(F32)
    chunk_ref[CHUNK:CHUNK + 1, :] = hi
    chunk_ref[CHUNK + 1:CHUNK + 2, :] = tap - hi
    mine = chunk_ref[...].astype(BF)
    for j in range(PEERS):
        out_ref[j] = mine


def place_kernel(mine_ref, theirs_ref, grad_ref, taps_ref, flat_ref):
    core = which_core()
    for ref, which in ((mine_ref, core), (theirs_ref, 1 - core)):
        start = pl.multiple_of(which * H, H)
        for j in range(PEERS):
            flat_ref[j * CHUNK:(j + 1) * CHUNK, :] = ref[j, 0:CHUNK, :].astype(F32)
        for b in range(D // 128):
            grad_ref[0, pl.ds(start, H), b * 128:(b + 1) * 128] = (
                flat_ref[b * H:(b + 1) * H, :].astype(BF))
    for j in range(KER * 6):
        k, b = divmod(j, 6)
        pair = mine_ref[j, CHUNK:, :].astype(F32) + theirs_ref[j, CHUNK:, :].astype(F32)
        taps_ref[k, :, b * 128:(b + 1) * 128] = pair[0:1] + pair[1:2]


def params(mib):
    return pltpu.CompilerParams(vmem_limit_bytes=mib * MIB)


def body(features, lengths, front_weight, pointwise, kernel, targets):
    ring = route(
        (8, 4, 2, 4, 2), lambda y, h, c, x, z: (y, h, c, (x + 1 if c == 0 else x - 1) % 4, z))
    pair = route(
        (8, 4, 2, 4, 2),
        lambda y, h, c, x, z: (y, h if c == 0 else (h + 2 * z - 1) % 4, c, x, 1 - z),
    )
    swap = route((8, 4, 2), lambda y, h, c: (y, h, 1 - c))
    cores = [list(range(c, 64, 2)) for c in range(2)]

    def along_x(a):
        return lax.ppermute(a, ("dp", "section"), ring)

    def along_z(a):
        return lax.ppermute(a, ("dp", "section"), pair)

    def to_core(a):
        return lax.ppermute(a, "dp", swap)

    def to_chips(a):
        return lax.all_to_all(a, "dp", 0, 0, axis_index_groups=cores)

    flat_taps = jnp.transpose(kernel, (1, 0, 2))

    def prepare(far, rows):
        return pl.pallas_call(
            functools.partial(prep_kernel, far),
            name="far" if far else "near",
            out_shape=jax.ShapeDtypeStruct((rows, D), BF),
            in_specs=[ANY, VMEM],
            out_specs=VMEM,
            scratch_shapes=[pltpu.SemaphoreType.DMA],
        )(pointwise, flat_taps)

    near, far = prepare(False, NEAR), prepare(True, FAR)
    begin = pl.pallas_call(
        front_kernel,
        name="front",
        out_shape=jax.ShapeDtypeStruct((START, D), BF),
        in_specs=[VMEM, VMEM, VMEM, SMEM],
        out_specs=VMEM,
    )(features, front_weight, targets, lengths)

    n1, n3, begin = lax.optimization_barrier((along_x(near), along_z(near), begin))
    f1, f3 = along_x(far), along_z(far)
    n2 = along_x(n1)
    n4 = along_z(n1[:H + TAPS])
    f4 = along_x(f3)
    n2, n4, f1 = lax.optimization_barrier((n2, n4, f1))
    n5 = along_z(n2)
    m1 = to_core(jnp.concatenate([n1[:H + TAPS], f1[:H]], axis=0))
    m2 = to_core(jnp.concatenate([n2[:H], n4], axis=0))
    g4, m5 = to_core(f4[:H + 8]), to_core(n5[:H])
    here = [near, far, n1, f1, n2, n3, f3, n4, f4, n5]
    there = [m1, m2, g4, m5]

    payload = pl.pallas_call(
        model_kernel,
        name="model",
        out_shape=jax.ShapeDtypeStruct((L, PAY, D), BF),
        in_specs=[VMEM] + [ANY] * 14,
        out_specs=VMEM,
        scratch_shapes=[
            pltpu.VMEM((L, D, D), BF),
            pltpu.VMEM((L, TAPS, D), BF),
            pltpu.VMEM((L, 8, D), F32),
            pltpu.VMEM((L, T, 128), F32),
            pltpu.VMEM((L, T + 16, D), F32),
            pltpu.VMEM((L, T, D), F32),
            pltpu.VMEM((L, T, D), BF),
            pltpu.VMEM((T + 16, D), F32),
            pltpu.VMEM((T, D), F32),
            pltpu.SemaphoreType.DMA((L,)),
            pltpu.SemaphoreType.DMA((L,)),
        ],
        compiler_params=params(28),
    )(begin, *here, *there)

    received = lax.all_to_all(
        payload, "section", 0, 0, axis_index_groups=[list(range(L))])

    lend = pl.pallas_call(
        lend_kernel,
        name="lend",
        out_shape=jax.ShapeDtypeStruct((ROWS, 128), BF),
        in_specs=[VMEM],
        out_specs=VMEM,
        compiler_params=params(24),
    )(received)
    parts = pl.pallas_call(
        grad_kernel,
        name="grad",
        out_shape=jax.ShapeDtypeStruct((PEERS, CROWS, 128), BF),
        in_specs=[VMEM, VMEM],
        out_specs=VMEM,
        scratch_shapes=[pltpu.VMEM((ROWS, 128), F32), pltpu.VMEM((CROWS, 128), F32)],
        compiler_params=params(24),
    )(received, to_core(lend))

    scattered = to_chips(parts)

    mine = pl.pallas_call(
        sum_kernel,
        name="total",
        out_shape=jax.ShapeDtypeStruct((PEERS, CROWS, 128), BF),
        in_specs=[VMEM],
        out_specs=VMEM,
        scratch_shapes=[pltpu.VMEM((CROWS, 128), F32)],
        compiler_params=params(16),
    )(scattered)

    half = to_chips(mine)
    other_half = to_core(half)

    grads, tap_grads = pl.pallas_call(
        place_kernel,
        name="place",
        out_shape=(
            jax.ShapeDtypeStruct((1, D, D), BF),
            jax.ShapeDtypeStruct((KER, 1, D), F32),
        ),
        in_specs=[VMEM, VMEM],
        out_specs=(VMEM, VMEM),
        scratch_shapes=[pltpu.VMEM((H * 6, 128), F32)],
        compiler_params=params(16),
    )(half, other_half)
    return grads, jnp.transpose(tap_grads, (1, 0, 2))


def solution(mesh):
    dp, section = "dp", "section"
    return jax.shard_map(
        body,
        mesh=mesh,
        in_specs=(
            P(dp, None, None),
            P(dp),
            P(),
            P(section, None, None),
            P(section, None, None),
            P(dp, None, None),
        ),
        out_specs=(P(section, None, None), P(section, None, None)),
        check_vma=False,
    )
```

```python
import functools
import itertools

import jax
import jax.numpy as jnp
from jax import lax
from jax.experimental import pallas as pl
from jax.experimental.pallas import tpu as pltpu
from jax.sharding import Mesh, PartitionSpec as P

EPS = 1e-06
BF = jnp.bfloat16
F32 = jnp.float32

D = 768
H = 384
KER = 5
FEAT = 512
T = 64
L = 8
TAPS = 16
NEAR = H + TAPS + 8
FAR = H + 2 * TAPS
START = 2 * T + 16
PAY = T + 8
ROWS = H * 6
PEERS = 32
CHUNK = 72
CROWS = 80
MIB = 1024 * 1024
BLOCKS = [slice(i, i + H) for i in range(0, D, H)]

VMEM = pl.BlockSpec(memory_space=pltpu.VMEM)
ANY = pl.BlockSpec(memory_space=pl.ANY)
SMEM = pl.BlockSpec(memory_space=pltpu.SMEM)


def route(shape, step):
    spots = list(itertools.product(*map(range, shape)))
    place = {spot: i for i, spot in enumerate(spots)}
    return [(place[spot], place[step(*spot)]) for spot in spots]


def split3(x):
    hi = x.astype(BF).astype(F32)
    rest = x - hi
    mid = rest.astype(BF).astype(F32)
    return hi, mid, rest - mid


def where_am_i():
    section = 2 * lax.axis_index("x") + lax.axis_index("zl")
    return section, lax.axis_index("c")


def prep_kernel(far, w_ref, taps_ref, out_ref, sem):
    core = lax.axis_index("c")
    part = pl.multiple_of((1 - core if far else core) * H, H)
    copy = pltpu.make_async_copy(w_ref.at[0, pl.ds(part, H)], out_ref.at[pl.ds(0, H)], sem)
    copy.start()
    taps = jnp.concatenate([taps_ref[k] for k in range(KER)], axis=0)
    hi, mid, low = split3(taps)
    packed = jnp.concatenate([hi, mid, low, jnp.zeros((1, D), F32)], axis=0).astype(BF)
    out_ref[H:H + TAPS, :] = packed
    out_ref[H + TAPS:, :] = jnp.zeros((out_ref.shape[0] - H - TAPS, D), BF)
    copy.wait()


def front_kernel(feat_ref, front_ref, targ_ref, len_ref, out_ref, input_ref, weight_ref, sem):
    section, _ = where_am_i()
    utt = lax.rem(section, 4)
    copies = [
        pltpu.make_async_copy(front_ref, weight_ref, sem.at[0]),
        pltpu.make_async_copy(feat_ref.at[utt], input_ref, sem.at[1]),
        pltpu.make_async_copy(targ_ref.at[utt], out_ref.at[pl.ds(T, T)], sem.at[2]),
    ]
    for copy in copies:
        copy.start()
    count = len_ref[utt].astype(F32)
    out_ref[2 * T:, :] = jnp.full((START - 2 * T, D), count, F32).astype(BF)
    for copy in copies:
        copy.wait()
    out_ref[0:T, :] = jnp.dot(
        input_ref[...], weight_ref[...], preferred_element_type=F32).astype(BF)


def model_kernel(
    start_ref,
    n0, f0, n1, f1, n2, n3, f3, n4, f4, n5, m1, m2, g4, m5,
    pay_ref,
    w_ref, traw_ref, taps_ref, inv_ref, norm_ref, slope_ref, act_ref, gpad_ref, g_ref,
    wsem, tsem,
):
    section, core = where_am_i()
    col = lax.div(section, 2)
    row = lax.rem(section, 2)
    other = 1 - core
    side = lax.rem(col + 3 + 2 * core, 4)
    anti = lax.rem(col + 1 + 2 * core, 4)
    across = lax.rem(col + 2, 4)
    flip = 1 - row

    def bring(piece, first, c, r, part, taps_at):
        layer = 2 * c + r
        start = pl.multiple_of(part * H, H)
        pltpu.make_async_copy(
            piece.at[pl.ds(first, H)], w_ref.at[layer, pl.ds(start, H)], wsem.at[layer]).start()
        if taps_at is not None:
            pltpu.make_async_copy(
                piece.at[pl.ds(taps_at, TAPS)], traw_ref.at[layer], tsem.at[layer]).start()

    for near, far, c, r in (
        (n0, f0, col, row), (n1, f1, side, row), (n3, f3, col, flip), (n4, f4, side, flip),
    ):
        bring(near, 0, c, r, core, H)
        bring(far, 0, c, r, other, None)
    bring(m1, 0, anti, row, other, H)
    bring(m1, H + TAPS, anti, row, core, None)
    bring(m2, H, anti, flip, other, 2 * H)
    bring(g4, 0, anti, flip, core, None)
    bring(n2, 0, across, row, core, H)
    bring(m2, 0, across, row, other, None)
    bring(n5, 0, across, flip, core, H)
    bring(m5, 0, across, flip, other, None)

    count = start_ref[2 * T:, :].astype(F32)[0:1, 0:1]
    target = start_ref[T:2 * T, :].astype(F32)
    frame = lax.broadcasted_iota(jnp.int32, (T, 1), 0).astype(F32)
    mask = jnp.where(frame < count, 1.0, 0.0).astype(F32)
    g_ref[...] = start_ref[0:T, :].astype(F32)

    edge = jnp.zeros((8, D), F32)
    gpad_ref[0:8, :] = edge
    gpad_ref[T + 8:, :] = edge

    def forward(l, carry):
        pltpu.make_async_copy(traw_ref.at[l], traw_ref.at[l], tsem.at[l]).wait()
        pltpu.make_async_copy(w_ref.at[l], w_ref.at[l], wsem.at[l]).wait()
        raw = traw_ref[l].astype(F32)
        taps = raw[0:KER] + raw[KER:2 * KER] + raw[2 * KER:3 * KER]
        taps_ref[l, 0:KER, :] = taps
        vals = g_ref[...]
        inv = lax.rsqrt(jnp.mean(vals * vals, axis=-1, keepdims=True) + EPS)
        inv_ref[l] = jnp.broadcast_to(inv, (T, 128))
        scale = inv * mask
        norm_ref[l, 0:8, :] = edge
        norm_ref[l, T + 8:, :] = edge
        out = vals
        for block in BLOCKS:
            norm_ref[l, 8:T + 8, block] = vals[:, block] * scale
            conv = taps[0:1, block] * norm_ref[l, 6:T + 6, block]
            for k in range(1, KER):
                conv = conv + taps[k:k + 1, block] * norm_ref[l, 6 + k:T + 6 + k, block]
            sig = jax.nn.sigmoid(conv)
            act = (conv * sig).astype(BF)
            slope_ref[l, :, block] = sig * (1.0 + conv * (1.0 - sig))
            act_ref[l, :, block] = act
            out = out + jnp.dot(act, w_ref[l, block, :], preferred_element_type=F32)
        g_ref[...] = out.astype(BF).astype(F32)
        return carry

    lax.fori_loop(0, L, forward, 0, unroll=True)

    g_ref[...] = ((g_ref[...] - target) * mask / count).astype(BF).astype(F32)

    first = section < 4

    def backward(i, carry):
        l = L - 1 - i
        g = g_ref[...]
        gb = g.astype(BF)
        pay_ref[l, 0:T, :] = jnp.where(first, act_ref[l].astype(F32), g).astype(BF)
        inv = inv_ref[l][:, 0:1]
        taps = taps_ref[l, 0:KER, :]
        grads, mean = [], 0.0
        for block in BLOCKS:
            grad_act = lax.dot_general(
                gb, w_ref[l, block, :], (((1,), (1,)), ((), ())), preferred_element_type=F32)
            grad_conv = grad_act * slope_ref[l, :, block]
            gpad_ref[8:T + 8, block] = grad_conv
            rows = []
            for k in range(KER):
                rows.append(jnp.sum(
                    grad_conv * norm_ref[l, 6 + k:T + 6 + k, block], axis=0, keepdims=True))
            total = jnp.concatenate(rows, axis=0)
            hi = total.astype(BF).astype(F32)
            part = jnp.where(first, hi, total - hi)
            part = jnp.concatenate([part, jnp.zeros((8 - KER, part.shape[1]), F32)], axis=0)
            pay_ref[l, T:, block] = part.astype(BF)
            grad_norm = taps[0:1, block] * gpad_ref[10:T + 10, block]
            for k in range(1, KER):
                grad_norm = grad_norm + taps[k:k + 1, block] * gpad_ref[10 - k:T + 10 - k, block]
            grad_norm = grad_norm * mask
            grads.append(grad_norm)
            mean = mean + jnp.sum(
                grad_norm * norm_ref[l, 8:T + 8, block], axis=-1, keepdims=True)
        mean = mean * (1.0 / D)
        for block, grad_norm in zip(BLOCKS, grads):
            norm = norm_ref[l, 8:T + 8, block]
            g_ref[:, block] = (
                g[:, block] + inv * (grad_norm - norm * mean)).astype(BF).astype(F32)
        return carry

    lax.fori_loop(0, L, backward, 0, unroll=True)


def half_product(recv_ref, part, out_ref):
    start = pl.multiple_of(part * H, H)
    act = recv_ref[0:4, 0:T, pl.ds(start, H)].reshape(4 * T, H)
    cot = recv_ref[4:8, 0:T, :].reshape(4 * T, D)
    grad = lax.dot_general(act, cot, (((0,), (0,)), ((), ())), preferred_element_type=F32)
    for b in range(D // 128):
        out_ref[b * H:(b + 1) * H, :] = grad[:, b * 128:(b + 1) * 128].astype(out_ref.dtype)


def lend_kernel(recv_ref, out_ref):
    half_product(recv_ref, 1 - lax.axis_index("c"), out_ref)


def grad_kernel(recv_ref, lent_ref, out_ref, flat_ref, chunk_ref):
    half_product(recv_ref, lax.axis_index("c"), flat_ref)
    taps = recv_ref[0, T:, :].astype(F32)
    for i in range(1, L):
        taps = taps + recv_ref[i, T:, :].astype(F32)
    total = taps[0:KER]
    hi = total.astype(BF).astype(F32)
    low = total - hi
    chunk_ref[CHUNK:, :] = jnp.zeros((CROWS - CHUNK, 128), F32)
    flat_ref[...] = flat_ref[...] + lent_ref[...].astype(F32)
    for j in range(PEERS):
        chunk_ref[0:CHUNK, :] = flat_ref[j * CHUNK:(j + 1) * CHUNK, :]
        if j < KER * 6:
            k, b = divmod(j, 6)
            chunk_ref[CHUNK:CHUNK + 1, :] = hi[k:k + 1, b * 128:(b + 1) * 128]
            chunk_ref[CHUNK + 1:CHUNK + 2, :] = low[k:k + 1, b * 128:(b + 1) * 128]
        out_ref[j] = chunk_ref[...].astype(BF)


def sum_kernel(parts_ref, out_ref, chunk_ref):
    total = parts_ref[0].astype(F32)
    for j in range(1, PEERS):
        total = total + parts_ref[j].astype(F32)
    chunk_ref[...] = total
    tap = total[CHUNK:CHUNK + 1] + total[CHUNK + 1:CHUNK + 2]
    hi = tap.astype(BF).astype(F32)
    chunk_ref[CHUNK:CHUNK + 1, :] = hi
    chunk_ref[CHUNK + 1:CHUNK + 2, :] = tap - hi
    mine = chunk_ref[...].astype(BF)
    for j in range(PEERS):
        out_ref[j] = mine


def place_kernel(mine_ref, theirs_ref, grad_ref, taps_ref, flat_ref):
    core = lax.axis_index("c")
    for ref, which in ((mine_ref, core), (theirs_ref, 1 - core)):
        start = pl.multiple_of(which * H, H)
        for j in range(PEERS):
            flat_ref[j * CHUNK:(j + 1) * CHUNK, :] = ref[j, 0:CHUNK, :].astype(F32)
        for b in range(D // 128):
            grad_ref[0, pl.ds(start, H), b * 128:(b + 1) * 128] = (
                flat_ref[b * H:(b + 1) * H, :].astype(BF))
    for j in range(KER * 6):
        k, b = divmod(j, 6)
        pair = mine_ref[j, CHUNK:, :].astype(F32) + theirs_ref[j, CHUNK:, :].astype(F32)
        taps_ref[k, :, b * 128:(b + 1) * 128] = pair[0:1] + pair[1:2]


def params(mib):
    return pltpu.CompilerParams(vmem_limit_bytes=mib * MIB)


def body(features, lengths, front_weight, pointwise, kernel, targets):
    ring = route((2, 4), lambda c, x: (c, (x + 1 if c == 0 else x - 1) % 4))
    pair = route(
        (4, 2, 2),
        lambda h, c, z: (h, c, 1 - z) if c == 0 else ((h + 2 * z - 1) % 4, c, 1 - z),
    )

    def along_x(a):
        return lax.ppermute(a, ("c", "x"), ring)

    def along_z(a):
        return lax.ppermute(a, ("zh", "c", "zl"), pair)

    def to_core(a):
        return lax.ppermute(a, "c", [(0, 1), (1, 0)])

    flat_taps = jnp.transpose(kernel, (1, 0, 2))

    def prepare(far, rows):
        return pl.pallas_call(
            functools.partial(prep_kernel, far),
            name="far" if far else "near",
            out_shape=jax.ShapeDtypeStruct((rows, D), BF),
            in_specs=[ANY, VMEM],
            out_specs=VMEM,
            scratch_shapes=[pltpu.SemaphoreType.DMA],
        )(pointwise, flat_taps)

    near, far = prepare(False, NEAR), prepare(True, FAR)
    begin = pl.pallas_call(
        front_kernel,
        name="front",
        out_shape=jax.ShapeDtypeStruct((START, D), BF),
        in_specs=[ANY, ANY, ANY, SMEM],
        out_specs=VMEM,
        scratch_shapes=[
            pltpu.VMEM((T, FEAT), BF),
            pltpu.VMEM((FEAT, D), BF),
            pltpu.SemaphoreType.DMA((3,)),
        ],
    )(features, front_weight, targets, lengths)

    n1, n3, begin = lax.optimization_barrier((along_x(near), along_z(near), begin))
    f1, f3 = along_x(far), along_z(far)
    n2 = along_x(n1)
    n4 = along_z(n1[:H + TAPS])
    f4 = along_x(f3)
    n2, n4, f1 = lax.optimization_barrier((n2, n4, f1))
    n5 = along_z(n2)
    m1 = to_core(jnp.concatenate([n1[:H + TAPS], f1[:H]], axis=0))
    m2 = to_core(jnp.concatenate([n2[:H], n4], axis=0))
    g4, m5 = to_core(f4[:H + 8]), to_core(n5[:H])
    here = [near, far, n1, f1, n2, n3, f3, n4, f4, n5]
    there = [m1, m2, g4, m5]

    payload = pl.pallas_call(
        model_kernel,
        name="model",
        out_shape=jax.ShapeDtypeStruct((L, PAY, D), BF),
        in_specs=[VMEM] + [ANY] * 14,
        out_specs=VMEM,
        scratch_shapes=[
            pltpu.VMEM((L, D, D), BF),
            pltpu.VMEM((L, TAPS, D), BF),
            pltpu.VMEM((L, 8, D), F32),
            pltpu.VMEM((L, T, 128), F32),
            pltpu.VMEM((L, T + 16, D), F32),
            pltpu.VMEM((L, T, D), F32),
            pltpu.VMEM((L, T, D), BF),
            pltpu.VMEM((T + 16, D), F32),
            pltpu.VMEM((T, D), F32),
            pltpu.SemaphoreType.DMA((L,)),
            pltpu.SemaphoreType.DMA((L,)),
        ],
        compiler_params=params(28),
    )(begin, *here, *there)

    received = lax.all_to_all(payload, ("x", "zl"), 0, 0)

    lend = pl.pallas_call(
        lend_kernel,
        name="lend",
        out_shape=jax.ShapeDtypeStruct((ROWS, 128), BF),
        in_specs=[VMEM],
        out_specs=VMEM,
        compiler_params=params(24),
    )(received)
    parts = pl.pallas_call(
        grad_kernel,
        name="grad",
        out_shape=jax.ShapeDtypeStruct((PEERS, CROWS, 128), BF),
        in_specs=[VMEM, VMEM],
        out_specs=VMEM,
        scratch_shapes=[pltpu.VMEM((ROWS, 128), F32), pltpu.VMEM((CROWS, 128), F32)],
        compiler_params=params(24),
    )(received, to_core(lend))

    scattered = lax.all_to_all(parts, ("y", "zh"), 0, 0)

    mine = pl.pallas_call(
        sum_kernel,
        name="total",
        out_shape=jax.ShapeDtypeStruct((PEERS, CROWS, 128), BF),
        in_specs=[VMEM],
        out_specs=VMEM,
        scratch_shapes=[pltpu.VMEM((CROWS, 128), F32)],
        compiler_params=params(16),
    )(scattered)

    half = lax.all_to_all(mine, ("y", "zh"), 0, 0)
    other_half = to_core(half)

    grads, tap_grads = pl.pallas_call(
        place_kernel,
        name="place",
        out_shape=(
            jax.ShapeDtypeStruct((1, D, D), BF),
            jax.ShapeDtypeStruct((KER, 1, D), F32),
        ),
        in_specs=[VMEM, VMEM],
        out_specs=(VMEM, VMEM),
        scratch_shapes=[pltpu.VMEM((H * 6, 128), F32)],
        compiler_params=params(16),
    )(half, other_half)
    return grads, jnp.transpose(tap_grads, (1, 0, 2))


def solution(mesh):
    fine = Mesh(mesh.devices.reshape(8, 4, 2, 4, 2), ("y", "zh", "c", "x", "zl"))
    dp = ("y", "zh", "c")
    section = ("x", "zl")
    return jax.shard_map(
        body,
        mesh=fine,
        in_specs=(
            P(dp, None, None),
            P(dp),
            P(),
            P(section, None, None),
            P(section, None, None),
            P(dp, None, None),
        ),
        out_specs=(P(section, None, None), P(section, None, None)),
        check_vma=False,
    )
```

```python
import itertools

import jax
import jax.numpy as jnp
from jax import lax
from jax.experimental import pallas as pl
from jax.experimental.pallas import tpu as pltpu
from jax.sharding import Mesh, PartitionSpec as P

EPS = 1e-06
BF = jnp.bfloat16
F32 = jnp.float32

D = 768
H = 384
KER = 5
FEAT = 512
T = 64
L = 8
TAPS = 16
NEAR = H + TAPS + 8
FAR = H + 2 * TAPS
START = 2 * T + 16
PAY = T + 8
ROWS = H * 6
PEERS = 32
CHUNK = 72
CROWS = 80
MIB = 1024 * 1024
BLOCKS = [slice(i, i + H) for i in range(0, D, H)]

VMEM = pl.BlockSpec(memory_space=pltpu.VMEM)
ANY = pl.BlockSpec(memory_space=pl.ANY)
SMEM = pl.BlockSpec(memory_space=pltpu.SMEM)


def route(shape, step):
    spots = list(itertools.product(*map(range, shape)))
    place = {spot: i for i, spot in enumerate(spots)}
    return [(place[spot], place[step(*spot)]) for spot in spots]


def split3(x):
    hi = x.astype(BF).astype(F32)
    rest = x - hi
    mid = rest.astype(BF).astype(F32)
    return hi, mid, rest - mid


def where_am_i():
    section = 2 * lax.axis_index("x") + lax.axis_index("zl")
    return section, lax.axis_index("c")


def prep_kernel(w_ref, taps_ref, near_ref, far_ref, sem):
    _, core = where_am_i()
    mine = pl.multiple_of(core * H, H)
    theirs = pl.multiple_of((1 - core) * H, H)
    copies = [
        pltpu.make_async_copy(w_ref.at[0, pl.ds(mine, H)], near_ref.at[pl.ds(0, H)], sem.at[0]),
        pltpu.make_async_copy(w_ref.at[0, pl.ds(theirs, H)], far_ref.at[pl.ds(0, H)], sem.at[1]),
    ]
    for copy in copies:
        copy.start()
    taps = jnp.concatenate([taps_ref[k] for k in range(KER)], axis=0)
    hi, mid, low = split3(taps)
    packed = jnp.concatenate([hi, mid, low, jnp.zeros((1, D), F32)], axis=0).astype(BF)
    near_ref[H:H + TAPS, :] = packed
    near_ref[H + TAPS:, :] = jnp.zeros((NEAR - H - TAPS, D), BF)
    far_ref[H:H + TAPS, :] = packed
    far_ref[H + TAPS:, :] = packed
    for copy in copies:
        copy.wait()


def front_kernel(feat_ref, front_ref, targ_ref, len_ref, out_ref):
    section, _ = where_am_i()
    utt = lax.rem(section, 4)
    out_ref[0:T, :] = jnp.dot(
        feat_ref[utt], front_ref[...], preferred_element_type=F32).astype(BF)
    out_ref[T:2 * T, :] = targ_ref[utt]
    count = len_ref[utt].astype(F32)
    out_ref[2 * T:, :] = jnp.full((START - 2 * T, D), count, F32).astype(BF)


def model_kernel(
    start_ref,
    n0, f0, n1, f1, n2, n3, f3, n4, f4, n5, m1, m2, g4, m5,
    pay_ref,
    w_ref, traw_ref, taps_ref, inv_ref, norm_ref, slope_ref, act_ref, gpad_ref, g_ref,
    wsem, tsem,
):
    section, core = where_am_i()
    col = lax.div(section, 2)
    row = lax.rem(section, 2)
    other = 1 - core
    side = lax.rem(col + 3 + 2 * core, 4)
    anti = lax.rem(col + 1 + 2 * core, 4)
    across = lax.rem(col + 2, 4)
    flip = 1 - row

    def bring(piece, first, c, r, part, taps_at):
        layer = 2 * c + r
        start = pl.multiple_of(part * H, H)
        pltpu.make_async_copy(
            piece.at[pl.ds(first, H)], w_ref.at[layer, pl.ds(start, H)], wsem.at[layer]).start()
        if taps_at is not None:
            pltpu.make_async_copy(
                piece.at[pl.ds(taps_at, TAPS)], traw_ref.at[layer], tsem.at[layer]).start()

    for near, far, c, r in (
        (n0, f0, col, row), (n1, f1, side, row), (n3, f3, col, flip), (n4, f4, side, flip),
    ):
        bring(near, 0, c, r, core, H)
        bring(far, 0, c, r, other, None)
    bring(m1, 0, anti, row, other, H)
    bring(m1, H + TAPS, anti, row, core, None)
    bring(m2, H, anti, flip, other, 2 * H)
    bring(g4, 0, anti, flip, core, None)
    bring(n2, 0, across, row, core, H)
    bring(m2, 0, across, row, other, None)
    bring(n5, 0, across, flip, core, H)
    bring(m5, 0, across, flip, other, None)

    count = start_ref[2 * T:, :].astype(F32)[0:1, 0:1]
    target = start_ref[T:2 * T, :].astype(F32)
    frame = lax.broadcasted_iota(jnp.int32, (T, 1), 0).astype(F32)
    mask = jnp.where(frame < count, 1.0, 0.0).astype(F32)
    g_ref[...] = start_ref[0:T, :].astype(F32)

    edge = jnp.zeros((8, D), F32)
    gpad_ref[0:8, :] = edge
    gpad_ref[T + 8:, :] = edge

    def forward(l, carry):
        pltpu.make_async_copy(traw_ref.at[l], traw_ref.at[l], tsem.at[l]).wait()
        pltpu.make_async_copy(w_ref.at[l], w_ref.at[l], wsem.at[l]).wait()
        raw = traw_ref[l].astype(F32)
        taps = raw[0:KER] + raw[KER:2 * KER] + raw[2 * KER:3 * KER]
        taps_ref[l, 0:KER, :] = taps
        vals = g_ref[...]
        inv = lax.rsqrt(jnp.mean(vals * vals, axis=-1, keepdims=True) + EPS)
        inv_ref[l] = jnp.broadcast_to(inv, (T, 128))
        scale = inv * mask
        norm_ref[l, 0:8, :] = edge
        norm_ref[l, T + 8:, :] = edge
        out = vals
        for block in BLOCKS:
            norm_ref[l, 8:T + 8, block] = vals[:, block] * scale
            conv = taps[0:1, block] * norm_ref[l, 6:T + 6, block]
            for k in range(1, KER):
                conv = conv + taps[k:k + 1, block] * norm_ref[l, 6 + k:T + 6 + k, block]
            sig = jax.nn.sigmoid(conv)
            act = (conv * sig).astype(BF)
            slope_ref[l, :, block] = sig * (1.0 + conv * (1.0 - sig))
            act_ref[l, :, block] = act
            out = out + jnp.dot(act, w_ref[l, block, :], preferred_element_type=F32)
        g_ref[...] = out.astype(BF).astype(F32)
        return carry

    lax.fori_loop(0, L, forward, 0, unroll=True)

    g_ref[...] = ((g_ref[...] - target) * mask / count).astype(BF).astype(F32)

    first = section < 4

    def backward(i, carry):
        l = L - 1 - i
        g = g_ref[...]
        gb = g.astype(BF)
        pay_ref[l, 0:T, :] = jnp.where(first, act_ref[l].astype(F32), g).astype(BF)
        inv = inv_ref[l][:, 0:1]
        taps = taps_ref[l, 0:KER, :]
        grads, mean = [], 0.0
        for block in BLOCKS:
            grad_act = lax.dot_general(
                gb, w_ref[l, block, :], (((1,), (1,)), ((), ())), preferred_element_type=F32)
            grad_conv = grad_act * slope_ref[l, :, block]
            gpad_ref[8:T + 8, block] = grad_conv
            rows = []
            for k in range(KER):
                rows.append(jnp.sum(
                    grad_conv * norm_ref[l, 6 + k:T + 6 + k, block], axis=0, keepdims=True))
            total = jnp.concatenate(rows, axis=0)
            hi = total.astype(BF).astype(F32)
            part = jnp.where(first, hi, total - hi)
            part = jnp.concatenate([part, jnp.zeros((8 - KER, part.shape[1]), F32)], axis=0)
            pay_ref[l, T:, block] = part.astype(BF)
            grad_norm = taps[0:1, block] * gpad_ref[10:T + 10, block]
            for k in range(1, KER):
                grad_norm = grad_norm + taps[k:k + 1, block] * gpad_ref[10 - k:T + 10 - k, block]
            grad_norm = grad_norm * mask
            grads.append(grad_norm)
            mean = mean + jnp.sum(
                grad_norm * norm_ref[l, 8:T + 8, block], axis=-1, keepdims=True)
        mean = mean * (1.0 / D)
        for block, grad_norm in zip(BLOCKS, grads):
            norm = norm_ref[l, 8:T + 8, block]
            g_ref[:, block] = (
                g[:, block] + inv * (grad_norm - norm * mean)).astype(BF).astype(F32)
        return carry

    lax.fori_loop(0, L, backward, 0, unroll=True)


def half_product(recv_ref, part, out_ref):
    start = pl.multiple_of(part * H, H)
    act = recv_ref[0:4, 0:T, pl.ds(start, H)].reshape(4 * T, H)
    cot = recv_ref[4:8, 0:T, :].reshape(4 * T, D)
    grad = lax.dot_general(act, cot, (((0,), (0,)), ((), ())), preferred_element_type=F32)
    for b in range(D // 128):
        out_ref[b * H:(b + 1) * H, :] = grad[:, b * 128:(b + 1) * 128].astype(out_ref.dtype)


def lend_kernel(recv_ref, out_ref):
    half_product(recv_ref, 1 - lax.axis_index("c"), out_ref)


def grad_kernel(recv_ref, lent_ref, out_ref, flat_ref, chunk_ref):
    half_product(recv_ref, lax.axis_index("c"), flat_ref)
    taps = recv_ref[0, T:, :].astype(F32)
    for i in range(1, L):
        taps = taps + recv_ref[i, T:, :].astype(F32)
    total = taps[0:KER]
    hi = total.astype(BF).astype(F32)
    low = total - hi
    chunk_ref[CHUNK:, :] = jnp.zeros((CROWS - CHUNK, 128), F32)
    flat_ref[...] = flat_ref[...] + lent_ref[...].astype(F32)
    for j in range(PEERS):
        chunk_ref[0:CHUNK, :] = flat_ref[j * CHUNK:(j + 1) * CHUNK, :]
        if j < KER * 6:
            k, b = divmod(j, 6)
            chunk_ref[CHUNK:CHUNK + 1, :] = hi[k:k + 1, b * 128:(b + 1) * 128]
            chunk_ref[CHUNK + 1:CHUNK + 2, :] = low[k:k + 1, b * 128:(b + 1) * 128]
        out_ref[j] = chunk_ref[...].astype(BF)


def sum_kernel(parts_ref, out_ref, chunk_ref):
    total = parts_ref[0].astype(F32)
    for j in range(1, PEERS):
        total = total + parts_ref[j].astype(F32)
    chunk_ref[...] = total
    tap = total[CHUNK:CHUNK + 1] + total[CHUNK + 1:CHUNK + 2]
    hi = tap.astype(BF).astype(F32)
    chunk_ref[CHUNK:CHUNK + 1, :] = hi
    chunk_ref[CHUNK + 1:CHUNK + 2, :] = tap - hi
    mine = chunk_ref[...].astype(BF)
    for j in range(PEERS):
        out_ref[j] = mine


def place_kernel(mine_ref, theirs_ref, grad_ref, taps_ref, flat_ref):
    core = lax.axis_index("c")
    for ref, which in ((mine_ref, core), (theirs_ref, 1 - core)):
        start = pl.multiple_of(which * H, H)
        for j in range(PEERS):
            flat_ref[j * CHUNK:(j + 1) * CHUNK, :] = ref[j, 0:CHUNK, :].astype(F32)
        for b in range(D // 128):
            grad_ref[0, pl.ds(start, H), b * 128:(b + 1) * 128] = (
                flat_ref[b * H:(b + 1) * H, :].astype(BF))
    for j in range(KER * 6):
        k, b = divmod(j, 6)
        pair = mine_ref[j, CHUNK:, :].astype(F32) + theirs_ref[j, CHUNK:, :].astype(F32)
        taps_ref[k, :, b * 128:(b + 1) * 128] = pair[0:1] + pair[1:2]


def params(mib):
    return pltpu.CompilerParams(vmem_limit_bytes=mib * MIB)


def body(features, lengths, front_weight, pointwise, kernel, targets):
    ring = route((2, 4), lambda c, x: (c, (x + 1 if c == 0 else x - 1) % 4))
    pair = route(
        (4, 2, 2),
        lambda h, c, z: (h, c, 1 - z) if c == 0 else ((h + 2 * z - 1) % 4, c, 1 - z),
    )

    def along_x(a):
        return lax.ppermute(a, ("c", "x"), ring)

    def along_z(a):
        return lax.ppermute(a, ("zh", "c", "zl"), pair)

    def to_core(a):
        return lax.ppermute(a, "c", [(0, 1), (1, 0)])

    near, far = pl.pallas_call(
        prep_kernel,
        name="prep",
        out_shape=(jax.ShapeDtypeStruct((NEAR, D), BF), jax.ShapeDtypeStruct((FAR, D), BF)),
        in_specs=[ANY, VMEM],
        out_specs=(VMEM, VMEM),
        scratch_shapes=[pltpu.SemaphoreType.DMA((2,))],
    )(pointwise, jnp.transpose(kernel, (1, 0, 2)))
    begin = pl.pallas_call(
        front_kernel,
        name="front",
        out_shape=jax.ShapeDtypeStruct((START, D), BF),
        in_specs=[VMEM, VMEM, VMEM, SMEM],
        out_specs=VMEM,
    )(features, front_weight, targets, lengths)

    n1, n3, begin = lax.optimization_barrier((along_x(near), along_z(near), begin))
    f1, f3 = along_x(far), along_z(far)
    n2 = along_x(n1)
    n4 = along_z(n1[:H + TAPS])
    f4 = along_x(f3)
    n2, n4, f1 = lax.optimization_barrier((n2, n4, f1))
    n5 = along_z(n2)
    m1 = to_core(jnp.concatenate([n1[:H + TAPS], f1[:H]], axis=0))
    m2 = to_core(jnp.concatenate([n2[:H], n4], axis=0))
    g4, m5 = to_core(f4[:H + 8]), to_core(n5[:H])
    here = [near, far, n1, f1, n2, n3, f3, n4, f4, n5]
    there = [m1, m2, g4, m5]

    payload = pl.pallas_call(
        model_kernel,
        name="model",
        out_shape=jax.ShapeDtypeStruct((L, PAY, D), BF),
        in_specs=[VMEM] + [ANY] * 14,
        out_specs=VMEM,
        scratch_shapes=[
            pltpu.VMEM((L, D, D), BF),
            pltpu.VMEM((L, TAPS, D), BF),
            pltpu.VMEM((L, 8, D), F32),
            pltpu.VMEM((L, T, 128), F32),
            pltpu.VMEM((L, T + 16, D), F32),
            pltpu.VMEM((L, T, D), F32),
            pltpu.VMEM((L, T, D), BF),
            pltpu.VMEM((T + 16, D), F32),
            pltpu.VMEM((T, D), F32),
            pltpu.SemaphoreType.DMA((L,)),
            pltpu.SemaphoreType.DMA((L,)),
        ],
        compiler_params=params(28),
    )(begin, *here, *there)

    received = lax.all_to_all(payload, ("x", "zl"), 0, 0)

    lend = pl.pallas_call(
        lend_kernel,
        name="lend",
        out_shape=jax.ShapeDtypeStruct((ROWS, 128), BF),
        in_specs=[VMEM],
        out_specs=VMEM,
        compiler_params=params(24),
    )(received)
    parts = pl.pallas_call(
        grad_kernel,
        name="grad",
        out_shape=jax.ShapeDtypeStruct((PEERS, CROWS, 128), BF),
        in_specs=[VMEM, VMEM],
        out_specs=VMEM,
        scratch_shapes=[pltpu.VMEM((ROWS, 128), F32), pltpu.VMEM((CROWS, 128), F32)],
        compiler_params=params(24),
    )(received, to_core(lend))

    scattered = lax.all_to_all(parts, ("y", "zh"), 0, 0)

    mine = pl.pallas_call(
        sum_kernel,
        name="total",
        out_shape=jax.ShapeDtypeStruct((PEERS, CROWS, 128), BF),
        in_specs=[VMEM],
        out_specs=VMEM,
        scratch_shapes=[pltpu.VMEM((CROWS, 128), F32)],
        compiler_params=params(16),
    )(scattered)

    half = lax.all_to_all(mine, ("y", "zh"), 0, 0)
    other_half = to_core(half)

    grads, tap_grads = pl.pallas_call(
        place_kernel,
        name="place",
        out_shape=(
            jax.ShapeDtypeStruct((1, D, D), BF),
            jax.ShapeDtypeStruct((KER, 1, D), F32),
        ),
        in_specs=[VMEM, VMEM],
        out_specs=(VMEM, VMEM),
        scratch_shapes=[pltpu.VMEM((H * 6, 128), F32)],
        compiler_params=params(16),
    )(half, other_half)
    return grads, jnp.transpose(tap_grads, (1, 0, 2))


def solution(mesh):
    fine = Mesh(mesh.devices.reshape(8, 4, 2, 4, 2), ("y", "zh", "c", "x", "zl"))
    dp = ("y", "zh", "c")
    section = ("x", "zl")
    return jax.shard_map(
        body,
        mesh=fine,
        in_specs=(
            P(dp, None, None),
            P(dp),
            P(),
            P(section, None, None),
            P(section, None, None),
            P(dp, None, None),
        ),
        out_specs=(P(section, None, None), P(section, None, None)),
        check_vma=False,
    )
```
